512 devices in a mesh: depth: 16 (over y, core), slab: 32 (over z, x).
Axes of the slice: x: 4, y: 8, z: 8, core: 2. Of those that a mesh axis runs over, the one named last changes fastest.
Arguments:
- slabs: float32 [16, 32, 4, 256, 256], P('depth', 'slab'), as said below
- incident: float32 [16, 8192, 256], P('depth', 'slab'), may hold values from -6 to 6
Outputs:
- down_field: float32 [16, 8192, 256], P('depth', 'slab')
- reflected: float32 [16, 8192, 256], P('depth', 'slab')
The draws below stay inside these ranges and needn't reach their ends.
Inputs may be any that keep to these rules, and one draw needn't show every extreme that they name: Reflection blocks have spectral norm below one half; transmission blocks have spectral norm below 2, and every star product of consecutive slabs within a group has reflection blocks of norm below one.
All inputs are finite; a program needn't handle non-finite values.
Results may differ from the reference program's by a relative error of at most 0.0003.
Values sent between devices are 32-bit elements; how exact they have to be, the bound alone decides.
A program may use at most 64 MiB of HBM per device.

```python
import jax
import jax.numpy as jnp
from jax import lax

M = 256
GROUPS = 16
SLABS = 32
SOURCES = 8192


def draw_slabs(key, part):
    keys = jax.random.split(jax.random.fold_in(key, 71), 6)
    shape = (GROUPS, SLABS, M, M)
    noise = [jnp.clip(jax.random.normal(keys[i], shape, jnp.float32), -4.0, 4.0) for i in range(4)]
    low = 0.88
    high = 0.99
    scale = M ** (-0.5)
    eye = jnp.eye(M, dtype=jnp.float32)
    diag_down = jnp.exp(jax.random.uniform(keys[4], (GROUPS, SLABS, M, 1), jnp.float32, jnp.log(low), jnp.log(high)))
    diag_up = jnp.exp(jax.random.uniform(keys[5], (GROUPS, SLABS, M, 1), jnp.float32, jnp.log(low), jnp.log(high)))
    refl = 0.1 * scale * noise[0]
    trans = eye * diag_down + 0.25 * scale * noise[1]
    back = 0.1 * scale * noise[2]
    upward = eye * diag_up + 0.25 * scale * noise[3]
    return jnp.stack([refl, trans, back, upward], axis=2)


def block_levels(stream_key, extent, cuts, low, high):
    gain = 1.0
    for position, blocks in cuts:
        draws = jax.random.uniform(jax.random.fold_in(jax.random.fold_in(stream_key, 6), position), (blocks,), jnp.float32, low / len(cuts), high / len(cuts))
        gain = gain * jnp.repeat(jnp.exp(draws), extent[position] // blocks).reshape((-1,) + (1,) * (len(extent) - 1 - position))
    return gain


def scatter_about(stream_key, shape, width, reach, cuts=(), held_as=jnp.bfloat16):
    result = jax.random.normal(stream_key, shape, jnp.float32) * width
    if len(cuts) > 0:
        result = block_levels(stream_key, shape, cuts, -0.22, 0.18) * result
    return jnp.clip(result, min=-reach, max=reach).astype(held_as)


def setup_inputs(seed: int = 0) -> dict:
    arg_keys = jax.random.split(jax.random.key(seed), 3)
    return {
        "slabs": draw_slabs(jax.random.fold_in(arg_keys[2], 71), 0),
        "incident": scatter_about(arg_keys[1], (GROUPS, SOURCES, M), 1.0, 6.0, ((0, 16), (1, 32)), jnp.float32),
    }


def matmul(left, right):
    return jnp.dot(left.astype(jnp.float32), right.astype(jnp.float32), precision=lax.Precision.HIGHEST, preferred_element_type=jnp.float32)

def times_transpose(rows, matrix):
    return lax.dot_general(rows.astype(jnp.float32), matrix.astype(jnp.float32), (((1,), (1,)), ((), ())), precision=lax.Precision.HIGHEST, preferred_element_type=jnp.float32)

def star(upper, lower):
    order = upper.shape[1]
    refl_a, trans_a, back_a, up_a = (upper[0], upper[1], upper[2], upper[3])
    refl_b, trans_b, back_b, up_b = (lower[0], lower[1], lower[2], lower[3])
    eye = jnp.eye(order, dtype=jnp.float32)
    system = eye - matmul(back_a, refl_b)
    right = jnp.concatenate([trans_a, matmul(back_a, up_b)], axis=1)
    solved = jnp.linalg.solve(system, right)
    first = solved[:, :order]
    second = solved[:, order:]
    refl = refl_a + matmul(up_a, matmul(refl_b, first))
    trans = matmul(trans_b, first)
    back = back_b + matmul(trans_b, second)
    upward = matmul(up_a, up_b + matmul(refl_b, second))
    return jnp.stack([refl, trans, back, upward])

def merge_group(group_slabs):

    def fold(index, carry):
        return star(carry, group_slabs[index])
    return lax.fori_loop(1, group_slabs.shape[0], fold, group_slabs[0])

def reference(slabs, incident):
    merged = lax.map(merge_group, slabs)

    def descend(arriving, items):
        blocks, injected = items
        field = injected + arriving
        return (times_transpose(field, blocks[1]), (field, times_transpose(field, blocks[0])))
    start = jnp.zeros(incident.shape[1:], jnp.float32)
    last, outs = lax.scan(descend, start, (merged, incident))
    return (outs[0], outs[1])
```

```python
import functools

import jax
import jax.numpy as jnp
from jax import lax
from jax.experimental import pallas as pl
from jax.experimental.pallas import tpu as pltpu
from jax.sharding import PartitionSpec as P

F32 = jnp.float32
BF16 = jnp.bfloat16
MESH = pl.DeviceIdType.MESH
DOUBLINGS = 16
CHUNKS = 8
LEVELS = 5
OWN = 8 * LEVELS
PARTNER = OWN + 4
BLOCKS = OWN + 5
FINAL_R = 8 * (LEVELS - 1) + 6
FINAL_T = FINAL_R + 1


def split(value):
    high = value.astype(BF16)
    return high, (value - high.astype(F32)).astype(BF16)


def dot(left, right):
    return jnp.dot(left, right, preferred_element_type=F32)


def split_dot(left, right):
    return dot(left[0], right[0]) + (dot(left[0], right[1]) + dot(left[1], right[0]))


def matmul(left, right):
    return split_dot(split(left), split(right))


def kernel(
    slabs, incident, down, bounced,
    buf, power, inverse, coupled, field, arrive, leave, handed, handing, extra, pair_t, own_t,
    load_sem, store_sem, tree_send, tree_recv, cast_send, cast_recv,
    chain_send, chain_recv, hand_send, hand_recv, extra_send, extra_recv, part_send, part_recv,
):
    slab = lax.axis_index("slab")
    depth = lax.axis_index("depth")
    x = lax.rem(slab, 4)
    z = lax.div(slab, 4)
    core = lax.rem(depth, 2)
    y = lax.div(depth, 2)
    chips = lax.axis_size("depth") // 2
    order = buf.shape[1]
    rows = field.shape[0] // CHUNKS
    band = order // CHUNKS

    loads = [
        pltpu.make_async_copy(slabs.at[0, 0, i], buf.at[OWN + i], load_sem.at[i]) for i in range(4)
    ]
    loads.append(pltpu.make_async_copy(incident.at[0], field, load_sem.at[4]))
    for load in loads:
        load.start()

    def at(px, pz):
        return lax.rem(pz + 16, 8) * 4 + lax.rem(px + 8, 4)

    rt_x = 1 - core
    qu_x = 2 + core
    root_z = 3

    barrier = pltpu.get_barrier_semaphore()

    def greet(**target):
        pl.semaphore_signal(barrier, inc=1, device_id=target, device_id_type=MESH)

    for px, pz in ((1, 0), (-1, 0), (2, 0), (0, 1), (0, -1), (0, 2), (0, -2), (1, 1), (-1, -1), (1, -1), (-1, 1)):
        greet(slab=at(x + px, z + pz))
    greet(depth=depth + 1 - 2 * core)

    @pl.when(y > 0)
    def _():
        greet(depth=depth - 2)

    @pl.when(y < chips - 1)
    def _():
        greet(depth=depth + 2)

    pl.semaphore_wait(barrier, 12 + (y > 0).astype(jnp.int32) + (y < chips - 1).astype(jnp.int32))

    def slot(level, pair, part):
        return level * 8 + pair * 2 + part

    outer = (x == 0) | (x == 3)
    on_rt = x == rt_x
    on_qu = x == qu_x
    z2 = lax.rem(z, 2)
    z4 = lax.rem(z, 4)
    mirror = at(3 - x, z)
    crossing2 = (on_qu & (z2 == 0)) | (on_rt & (z2 == 1))
    merged2 = (on_rt & (z2 == 0)) | (on_qu & (z2 == 1))
    inner3 = (on_qu & (z4 == 1)) | (on_rt & (z4 == 2))
    ahead3 = jnp.where(z4 < 2, 1, -1)
    root = on_rt & (z == root_z)
    source4 = (on_rt & ((z == 1) | (z == 5))) | (on_qu & (z == 2))
    true = x >= 0
    false = x < 0
    routes = [
        [(true, at(x + 1 - 2 * lax.rem(x, 2), z), 2)],
        [
            (jnp.logical_not(outer), jnp.where(core == 0, mirror, at(x + 2, z)), 2),
            (outer == (core == 0), at(x + 1 - 2 * lax.rem(x, 2), z), core),
        ],
        [
            (crossing2, mirror, 1),
            (crossing2, at(x, z + 1 - 2 * z2), 2),
        ],
        [
            (inner3, mirror, 1),
            (merged2, at(x, z + ahead3), jnp.where(inner3, 2, 0)),
        ],
        [
            (source4, at(rt_x, root_z), jnp.where(on_qu, 1, jnp.where(z == 1, 0, 2))),
        ],
    ]
    computes = [
        true,
        on_rt | on_qu,
        merged2,
        (on_rt & (z4 == 1)) | (on_qu & (z4 == 2)),
        root,
    ]
    local = [3, 1 - core, 0, 3, 3]

    def tree_copy(level, number, part, source):
        sends, target, pair = routes[level][number]
        return sends, pltpu.make_async_remote_copy(
            src_ref=buf.at[source],
            dst_ref=buf.at[slot(level, pair, part)],
            send_sem=tree_send.at[level, number, part],
            recv_sem=tree_recv.at[level, pair, part],
            device_id={"slab": target},
            device_id_type=MESH,
        )

    def send_part(level, part, source):
        for number in range(len(routes[level])):
            sends, copy = tree_copy(level, number, part, source)

            @pl.when(sends)
            def _():
                copy.start()

    def await_part(level, pair, part):
        pltpu.make_async_remote_copy(
            src_ref=buf.at[slot(level, pair, part)],
            dst_ref=buf.at[slot(level, pair, part)],
            send_sem=tree_send.at[level, 0, part],
            recv_sem=tree_recv.at[level, pair, part],
            device_id={"slab": slab},
            device_id_type=MESH,
        ).wait_recv()

    for load in loads[:4]:
        load.wait()
    odd = lax.rem(x, 2) == 1
    first_pair = jnp.where(odd, OWN, OWN + 2)
    add_pair = jnp.where(odd, OWN + 2, OWN)
    send_part(0, 0, first_pair)
    send_part(0, 1, first_pair + 1)

    def operand(level, pair, part):
        if level == 0:
            if pair == 2:
                return slot(0, 2, part)
            return (add_pair if pair == 0 else first_pair) + part
        own = slot(level - 1, 3, part)
        known = local[level]
        if isinstance(known, int):
            return own if known == pair else slot(level, pair, part)
        return jnp.where(known == pair, own, slot(level, pair, part))

    def arrived(level, pair, part):
        if level == 0:
            if pair == 2:
                await_part(0, 2, part)
            return
        known = local[level]
        if isinstance(known, int):
            if known != pair:
                await_part(level, pair, part)
            return

        @pl.when(known != pair)
        def _():
            await_part(level, pair, part)

    def merge(level):
        arrived(level, 1, 0)
        arrived(level, 2, 0)
        near = buf[operand(level, 1, 0)]
        far = split(buf[operand(level, 2, 0)])
        system = split_dot(split(near), far)
        ones = lax.broadcasted_iota(jnp.int32, (order, order), 0) == lax.broadcasted_iota(jnp.int32, (order, order), 1)
        inverse[...] = system + jnp.where(ones, 1.0, 0.0)
        power[...] = system

        def double(_, carry):
            halves = split(power[...])
            squared = split_dot(halves, halves)
            power[...] = squared
            whole = inverse[...]
            inverse[...] = whole + split_dot(split(squared), split(whole))
            return carry

        lax.fori_loop(0, DOUBLINGS - 1, double, 0)
        solved = split(inverse[...])
        coupled[...] = split_dot(far, solved)
        arrived(level, 0, 1)
        right = split(buf[operand(level, 0, 1)])
        through = split_dot(solved, right)
        turned = split_dot(split(coupled[...]), right)
        arrived(level, 1, 1)
        arrived(level, 0, 0)
        buf[slot(level, 3, 0)] = buf[operand(level, 0, 0)] + matmul(buf[operand(level, 1, 1)], turned)
        if level + 1 < LEVELS:
            send_part(level + 1, 0, slot(level, 3, 0))
        arrived(level, 2, 1)
        buf[slot(level, 3, 1)] = matmul(buf[operand(level, 2, 1)], through)
        if level + 1 < LEVELS:
            send_part(level + 1, 1, slot(level, 3, 1))

    for level in range(LEVELS):

        @pl.when(computes[level])
        def _(level=level):
            merge(level)

    dx = lax.rem(x - rt_x + 4, 4)
    dz = lax.rem(z - root_z + 8, 8)
    x_first = core == 0
    x_line = jnp.logical_not(x_first) | (dz == 0)
    z_line = x_first | (dx == 0)
    children = [
        (x_line & (dx <= 1), at(x + 1, z)),
        (x_line & (dx == 0), at(x - 1, z)),
        (z_line & (dz <= 3), at(x, z + 1)),
        (z_line & ((dz == 0) | (dz >= 6)), at(x, z - 1)),
    ]

    def cast_copy(which, chunk, child):
        place = buf.at[FINAL_R + which, pl.ds(chunk * band, band)]
        return pltpu.make_async_remote_copy(
            src_ref=place,
            dst_ref=place,
            send_sem=cast_send.at[which, chunk, child],
            recv_sem=cast_recv.at[which, chunk],
            device_id={"slab": children[child][1]},
            device_id_type=MESH,
        )

    def part_copy(chunk):
        return pltpu.make_async_remote_copy(
            src_ref=buf.at[FINAL_T, pl.ds(chunk * band, band)],
            dst_ref=buf.at[PARTNER, pl.ds(chunk * band, band)],
            send_sem=part_send.at[chunk],
            recv_sem=part_recv.at[chunk],
            device_id={"depth": depth + 1 - 2 * core},
            device_id_type=MESH,
        )

    def forward(which):
        for chunk in range(CHUNKS):

            @pl.when(jnp.logical_not(root))
            def _():
                cast_copy(which, chunk, 0).wait_recv()

            for child in range(4):

                @pl.when(children[child][0])
                def _():
                    cast_copy(which, chunk, child).start()

            if which == 1:

                @pl.when(core == 1)
                def _():
                    part_copy(chunk).start()

    forward(1)
    loads[4].wait()

    @pl.when((y > 0) | (core == 1))
    def _():
        forward(0)

    extra_copy = pltpu.make_async_remote_copy(
        src_ref=extra,
        dst_ref=extra,
        send_sem=extra_send,
        recv_sem=extra_recv,
        device_id={"depth": depth + 1 - 2 * core},
        device_id_type=MESH,
    )

    def keep_split(ref, value):
        ref[0], ref[1] = split(value)

    def chain_copy(chunk):
        return pltpu.make_async_remote_copy(
            src_ref=leave.at[pl.ds(chunk * rows, rows)],
            dst_ref=arrive.at[pl.ds(chunk * rows, rows)],
            send_sem=chain_send.at[chunk],
            recv_sem=chain_recv.at[chunk],
            device_id={"depth": lax.rem(depth + 2, 2 * chips)},
            device_id_type=MESH,
        )

    def hand_copy(chunk):
        return pltpu.make_async_remote_copy(
            src_ref=handing.at[pl.ds(chunk * rows, rows)],
            dst_ref=handed.at[pl.ds(chunk * rows, rows)],
            send_sem=hand_send.at[chunk],
            recv_sem=hand_recv.at[chunk],
            device_id={"depth": depth + 1 - 2 * core},
            device_id_type=MESH,
        )

    @pl.when(core == 1)
    def _():
        keep_split(own_t, buf[FINAL_T].T)
        extra[...] = split_dot(split(field[...]), (own_t[0], own_t[1]))
        extra_copy.start()
        for chunk in range(CHUNKS):
            part = pl.ds(chunk * rows, rows)
            hand_copy(chunk).wait_recv()
            field[part] += handed[part]

    @pl.when(core == 0)
    def _():
        keep_split(own_t, buf[FINAL_T].T)
        for chunk in range(CHUNKS):
            part_copy(chunk).wait_recv()
        keep_split(pair_t, matmul(buf[PARTNER], buf[FINAL_T]).T)
        extra_copy.wait_recv()
        for chunk in range(CHUNKS):
            part = pl.ds(chunk * rows, rows)

            @pl.when(y > 0)
            def _():
                chain_copy(chunk).wait_recv()
                field[part] += arrive[part]

            halves = split(field[part])

            @pl.when(y < chips - 1)
            def _():
                leave[part] = split_dot(halves, (pair_t[0], pair_t[1])) + extra[part]
                chain_copy(chunk).start()

            handing[part] = split_dot(halves, (own_t[0], own_t[1]))
            hand_copy(chunk).start()

    store_down = pltpu.make_async_copy(field, down.at[0], store_sem.at[0])
    store_down.start()

    @pl.when((y == 0) & (core == 0))
    def _():
        forward(0)

    arrive[...] = matmul(field[...], buf[FINAL_R].T)
    store_bounced = pltpu.make_async_copy(arrive, bounced.at[0], store_sem.at[1])
    store_bounced.start()

    for level in range(LEVELS):
        for number in range(len(routes[level])):
            for part in range(2):
                sends, copy = tree_copy(level, number, part, OWN)

                @pl.when(sends)
                def _():
                    copy.wait_send()

    for which in range(2):
        for chunk in range(CHUNKS):
            for child in range(4):

                @pl.when(children[child][0])
                def _():
                    cast_copy(which, chunk, child).wait_send()

    @pl.when(core == 1)
    def _():
        extra_copy.wait_send()
        for chunk in range(CHUNKS):
            part_copy(chunk).wait_send()

    @pl.when(core == 0)
    def _():
        for chunk in range(CHUNKS):
            hand_copy(chunk).wait_send()

        @pl.when(y < chips - 1)
        def _():
            for chunk in range(CHUNKS):
                chain_copy(chunk).wait_send()

    store_down.wait()
    store_bounced.wait()


def shards(slabs, incident):
    order = slabs.shape[-1]
    rows = incident.shape[1]
    block = jax.ShapeDtypeStruct(incident.shape, F32)
    matrix = pltpu.VMEM((order, order), F32)
    halves = pltpu.VMEM((2, order, order), BF16)
    fields = pltpu.VMEM((rows, order), F32)
    dma = pltpu.SemaphoreType.DMA
    return pl.pallas_call(
        kernel,
        out_shape=(block, block),
        in_specs=[pl.BlockSpec(memory_space=pl.ANY)] * 2,
        out_specs=[pl.BlockSpec(memory_space=pl.ANY)] * 2,
        scratch_shapes=[
            pltpu.VMEM((BLOCKS, order, order), F32),
            matrix, matrix, matrix,
            fields, fields, fields, fields, fields, fields,
            halves, halves,
            dma((5,)), dma((2,)),
            dma((LEVELS, 2, 2)), dma((LEVELS, 3, 2)),
            dma((2, CHUNKS, 4)), dma((2, CHUNKS)),
            dma((CHUNKS,)), dma((CHUNKS,)),
            dma((CHUNKS,)), dma((CHUNKS,)),
            dma, dma,
            dma((CHUNKS,)), dma((CHUNKS,)),
        ],
        compiler_params=pltpu.CompilerParams(collective_id=0, has_side_effects=True, vmem_limit_bytes=60 * 2**20),
        name="layers",
    )(slabs, incident)


def solution(mesh):
    placed = (P("depth", "slab", None, None, None), P("depth", "slab", None))
    return jax.shard_map(
        shards,
        mesh=mesh,
        in_specs=placed,
        out_specs=(P("depth", "slab", None), P("depth", "slab", None)),
        check_vma=False,
    )
```

```python
import functools

import jax
import jax.numpy as jnp
from jax import lax
from jax.experimental import pallas as pl
from jax.experimental.pallas import tpu as pltpu
from jax.sharding import PartitionSpec as P

F32 = jnp.float32
BF16 = jnp.bfloat16
MESH = pl.DeviceIdType.MESH
DOUBLINGS = 3
MORE_DOUBLINGS = 24
REMAINDER = 1e-6
CHUNKS = 8
CASTS = 8
ROOT_Z = 1
EARLY = 2
LEVELS = 5
OWN = 8 * LEVELS
PARTNER = OWN + 4
BLOCKS = OWN + 5
FINAL_R = 8 * (LEVELS - 1) + 6
FINAL_T = FINAL_R + 1


def split(value):
    high = value.astype(BF16)
    return high, (value - high.astype(F32)).astype(BF16)


def dot(left, right):
    return jnp.dot(left, right, preferred_element_type=F32)


def split_dot(left, right):
    return dot(left[0], right[0]) + (dot(left[0], right[1]) + dot(left[1], right[0]))


def matmul(left, right):
    return split_dot(split(left), split(right))


def kernel(
    doublings, slabs, incident, down, bounced, settled,
    buf, power, inverse, coupled, field, arrive, leave, handed, handing, extra, pair_t, bounce_t,
    load_sem, store_sem, tree_send, tree_recv, cast_send, cast_recv,
    chain_send, chain_recv, hand_send, hand_recv, extra_send, extra_recv, part_send, part_recv,
    heads, mark, head_send, head_recv,
):
    slab = lax.axis_index("slab")
    depth = lax.axis_index("depth")
    x = lax.rem(slab, 4)
    z = lax.div(slab, 4)
    core = lax.rem(depth, 2)
    y = lax.div(depth, 2)
    chips = lax.axis_size("depth") // 2
    order = buf.shape[1]
    rows = field.shape[0] // CHUNKS
    band = order // CASTS

    loads = [
        pltpu.make_async_copy(slabs.at[0, 0, i], buf.at[OWN + i], load_sem.at[i]) for i in range(4)
    ]
    loads.append(pltpu.make_async_copy(incident.at[0], field, load_sem.at[4]))
    for load in loads:
        load.start()

    def at(px, pz):
        return lax.rem(pz + 16, 8) * 4 + lax.rem(px + 8, 4)

    rt_x = 1 - core
    qu_x = 2 + core
    root_z = ROOT_Z

    def slot(level, pair, part):
        return level * 8 + pair * 2 + part

    outer = (x == 0) | (x == 3)
    on_rt = x == rt_x
    on_qu = x == qu_x
    z2 = lax.rem(z, 2)
    z4 = lax.rem(z, 4)
    mirror = at(3 - x, z)
    crossing2 = (on_qu & (z2 == 0)) | (on_rt & (z2 == 1))
    merged2 = (on_rt & (z2 == 0)) | (on_qu & (z2 == 1))
    inner3 = (on_qu & (z4 == 1)) | (on_rt & (z4 == 2))
    ahead3 = jnp.where(z4 < 2, 1, -1)
    root = on_rt & (z == root_z)
    rt_rows = [row for row in (1, 5) if row != root_z]
    sources = [(rt_x, row) for row in rt_rows] + [(qu_x, 2)]
    source4 = on_qu & (z == 2)
    for row in rt_rows:
        source4 = source4 | (on_rt & (z == row))

    barrier = pltpu.get_barrier_semaphore()

    def greet(**target):
        pl.semaphore_signal(barrier, inc=1, device_id=target, device_id_type=MESH)

    for px, pz in ((1, 0), (-1, 0), (2, 0), (0, 1), (0, -1)):
        greet(slab=at(x + px, z + pz))
    for step in range(1, 2 * chips):
        greet(depth=lax.rem(depth + step, 2 * chips))

    @pl.when(source4)
    def _():
        greet(slab=at(rt_x, root_z))

    @pl.when(root)
    def _():
        for px, pz in sources:
            greet(slab=at(px, pz))

    met = [source4] + [root] * len(sources)
    pl.semaphore_wait(barrier, 4 + 2 * chips + sum(flag.astype(jnp.int32) for flag in met))

    true = x >= 0
    false = x < 0
    routes = [
        [(true, at(x + 1 - 2 * lax.rem(x, 2), z), 2)],
        [
            (jnp.logical_not(outer), jnp.where(core == 0, mirror, at(x + 2, z)), 2),
            (outer == (core == 0), at(x + 1 - 2 * lax.rem(x, 2), z), core),
        ],
        [
            (crossing2, mirror, 1),
            (crossing2, at(x, z + 1 - 2 * z2), 2),
        ],
        [
            (inner3, mirror, 1),
            (merged2, at(x, z + ahead3), jnp.where(inner3, 2, 0)),
        ],
        [
            (source4, at(rt_x, root_z), jnp.where(on_qu, 1, jnp.where(z == 1, 0, 2))),
        ],
    ]
    computes = [
        true,
        on_rt | on_qu,
        merged2,
        (on_rt & (z4 == 1)) | (on_qu & (z4 == 2)),
        root,
    ]
    local = [3, 1 - core, 0, 3, {1: 0, 5: 2}.get(ROOT_Z, 3)]

    def tree_copy(level, number, part, source):
        sends, target, pair = routes[level][number]
        return sends, pltpu.make_async_remote_copy(
            src_ref=buf.at[source],
            dst_ref=buf.at[slot(level, pair, part)],
            send_sem=tree_send.at[level, number, part],
            recv_sem=tree_recv.at[level, pair, part],
            device_id={"slab": target},
            device_id_type=MESH,
        )

    def send_part(level, part, source):
        for number in range(len(routes[level])):
            sends, copy = tree_copy(level, number, part, source)

            @pl.when(sends)
            def _():
                copy.start()

    def await_part(level, pair, part):
        pltpu.make_async_remote_copy(
            src_ref=buf.at[slot(level, pair, part)],
            dst_ref=buf.at[slot(level, pair, part)],
            send_sem=tree_send.at[level, 0, part],
            recv_sem=tree_recv.at[level, pair, part],
            device_id={"slab": slab},
            device_id_type=MESH,
        ).wait_recv()

    for load in loads[:4]:
        load.wait()
    odd = lax.rem(x, 2) == 1
    first_pair = jnp.where(odd, OWN, OWN + 2)
    add_pair = jnp.where(odd, OWN + 2, OWN)
    send_part(0, 0, first_pair)
    send_part(0, 1, first_pair + 1)

    def operand(level, pair, part):
        if level == 0:
            if pair == 2:
                return slot(0, 2, part)
            return (add_pair if pair == 0 else first_pair) + part
        own = slot(level - 1, 3, part)
        known = local[level]
        if isinstance(known, int):
            return own if known == pair else slot(level, pair, part)
        return jnp.where(known == pair, own, slot(level, pair, part))

    def arrived(level, pair, part):
        if level == 0:
            if pair == 2:
                await_part(0, 2, part)
            return
        known = local[level]
        if isinstance(known, int):
            if known != pair:
                await_part(level, pair, part)
            return

        @pl.when(known != pair)
        def _():
            await_part(level, pair, part)

    def merge(level):
        arrived(level, 1, 0)
        arrived(level, 2, 0)
        near = buf[operand(level, 1, 0)]
        far = split(buf[operand(level, 2, 0)])
        system = split_dot(split(near), far)
        ones = lax.broadcasted_iota(jnp.int32, (order, order), 0) == lax.broadcasted_iota(jnp.int32, (order, order), 1)
        inverse[...] = system + jnp.where(ones, 1.0, 0.0)
        power[...] = system

        def double(halves):
            squared = split_dot(halves, halves)
            power[...] = squared
            whole = inverse[...]
            inverse[...] = whole + split_dot(split(squared), split(whole))

        if doublings <= DOUBLINGS:
            for _ in range(doublings - 1):
                double(split(power[...]))
            left = jnp.sum(jnp.square(power[...]), axis=(0, 1), keepdims=True)
            inverse[...] += jnp.where(left < REMAINDER, 0.0, jnp.nan)
        else:

            def step(_, carry):
                double(split(power[...]))
                return carry

            lax.fori_loop(0, doublings - 1, step, 0)
        solved = split(inverse[...])
        coupled[...] = split_dot(far, solved)
        arrived(level, 0, 1)
        right = split(buf[operand(level, 0, 1)])
        through = split_dot(solved, right)
        turned = split_dot(split(coupled[...]), right)
        arrived(level, 1, 1)
        arrived(level, 0, 0)
        buf[slot(level, 3, 0)] = buf[operand(level, 0, 0)] + matmul(buf[operand(level, 1, 1)], turned)
        if level + 1 < LEVELS:
            send_part(level + 1, 0, slot(level, 3, 0))
        arrived(level, 2, 1)
        buf[slot(level, 3, 1)] = matmul(buf[operand(level, 2, 1)], through)
        if level + 1 < LEVELS:
            send_part(level + 1, 1, slot(level, 3, 1))

    for level in range(LEVELS):

        @pl.when(computes[level])
        def _(level=level):
            merge(level)

    dx = lax.rem(x - rt_x + 4, 4)
    dz = lax.rem(z - root_z + 8, 8)
    x_first = core == 0
    x_line = jnp.logical_not(x_first) | (dz == 0)
    z_line = x_first | (dx == 0)
    children = [
        (x_line & ((dx == 0) | (x_first & (dx == 1))), at(x + 1, z)),
        (x_line & ((dx == 0) | (jnp.logical_not(x_first) & (dx == 3))), at(x - 1, z)),
        (z_line & (dz <= 3), at(x, z + 1)),
        (z_line & ((dz == 0) | (dz >= 6)), at(x, z - 1)),
    ]

    def cast_copy(which, chunk, child):
        place = buf.at[FINAL_R + which, pl.ds(chunk * band, band)]
        return pltpu.make_async_remote_copy(
            src_ref=place,
            dst_ref=place,
            send_sem=cast_send.at[which, chunk, child],
            recv_sem=cast_recv.at[which, chunk],
            device_id={"slab": children[child][1]},
            device_id_type=MESH,
        )

    def part_copy(chunk):
        return pltpu.make_async_remote_copy(
            src_ref=buf.at[FINAL_T, pl.ds(chunk * band, band)],
            dst_ref=buf.at[PARTNER, pl.ds(chunk * band, band)],
            send_sem=part_send.at[chunk],
            recv_sem=part_recv.at[chunk],
            device_id={"depth": depth + 1 - 2 * core},
            device_id_type=MESH,
        )

    def head_copy(step):
        return pltpu.make_async_remote_copy(
            src_ref=buf.at[FINAL_T, pl.ds(0, 8), pl.ds(0, 128)],
            dst_ref=heads.at[step],
            send_sem=head_send.at[step],
            recv_sem=head_recv.at[step],
            device_id={"depth": lax.rem(depth + step, 2 * chips)},
            device_id_type=MESH,
        )

    def forward(which):
        for chunk in range(CASTS):

            @pl.when(jnp.logical_not(root))
            def _():
                cast_copy(which, chunk, 0).wait_recv()

            for child in range(4):

                @pl.when(children[child][0])
                def _():
                    cast_copy(which, chunk, child).start()

            if which == 1:
                part_copy(chunk).start()
                if chunk == 0:
                    for step in range(1, 2 * chips):
                        head_copy(step).start()

    def keep_split(ref, value):
        ref[0], ref[1] = split(value)

    def kept(ref):
        return ref[0], ref[1]

    def forward_r():
        forward(0)
        keep_split(bounce_t, buf[FINAL_R].T)

    extra_copy = pltpu.make_async_remote_copy(
        src_ref=extra,
        dst_ref=extra,
        send_sem=extra_send,
        recv_sem=extra_recv,
        device_id={"depth": depth + 1 - 2 * core},
        device_id_type=MESH,
    )

    def chain_copy(chunk):
        return pltpu.make_async_remote_copy(
            src_ref=leave.at[pl.ds(chunk * rows, rows)],
            dst_ref=arrive.at[pl.ds(chunk * rows, rows)],
            send_sem=chain_send.at[chunk],
            recv_sem=chain_recv.at[chunk],
            device_id={"depth": lax.rem(depth + 2, 2 * chips)},
            device_id_type=MESH,
        )

    def hand_copy(chunk):
        return pltpu.make_async_remote_copy(
            src_ref=field.at[pl.ds(chunk * rows, rows)],
            dst_ref=handed.at[pl.ds(chunk * rows, rows)],
            send_sem=hand_send.at[chunk],
            recv_sem=hand_recv.at[chunk],
            device_id={"depth": depth + 1 - 2 * core},
            device_id_type=MESH,
        )

    forward(1)
    loads[4].wait()

    @pl.when(core == 1)
    def _():
        keep_split(pair_t, buf[FINAL_T].T)
        extra[...] = split_dot(split(field[...]), kept(pair_t))
        extra_copy.start()
        for chunk in range(CASTS):
            part_copy(chunk).wait_recv()
        keep_split(pair_t, buf[PARTNER].T)
        forward_r()
        for chunk in range(CHUNKS):
            part = pl.ds(chunk * rows, rows)
            hand_copy(chunk).wait_recv()
            field[part] += split_dot(split(handed[part]), kept(pair_t))

    @pl.when(core == 0)
    def _():
        for chunk in range(CASTS):
            part_copy(chunk).wait_recv()
        keep_split(pair_t, matmul(buf[PARTNER], buf[FINAL_T]).T)
        extra_copy.wait_recv()
        extra[...] += split_dot(split(field[...]), kept(pair_t))

        @pl.when(y == 0)
        def _():
            for chunk in range(CHUNKS):
                part = pl.ds(chunk * rows, rows)
                leave[part] = extra[part]
                chain_copy(chunk).start()
                hand_copy(chunk).start()

        @pl.when(y > EARLY)
        def _():
            forward_r()

        @pl.when(y > 0)
        def _():
            for chunk in range(CHUNKS):
                part = pl.ds(chunk * rows, rows)
                chain_copy(chunk).wait_recv()

                @pl.when(y < chips - 1)
                def _():
                    leave[part] = extra[part] + split_dot(split(arrive[part]), kept(pair_t))
                    chain_copy(chunk).start()

                field[part] += arrive[part]
                hand_copy(chunk).start()

        @pl.when(y <= EARLY)
        def _():
            forward_r()

    store_down = pltpu.make_async_copy(field, down.at[0], store_sem.at[0])
    store_down.start()

    handing[...] = split_dot(split(field[...]), kept(bounce_t))
    store_bounced = pltpu.make_async_copy(handing, bounced.at[0], store_sem.at[1])
    store_bounced.start()

    heads[0] = buf[FINAL_T, pl.ds(0, 8), pl.ds(0, 128)]
    for step in range(1, 2 * chips):
        head_copy(step).wait()
    mark[...] = sum(heads[step] for step in range(2 * chips)) * 0.0
    store_mark = pltpu.make_async_copy(mark, settled, store_sem.at[2])
    store_mark.start()

    for level in range(LEVELS):
        for number in range(len(routes[level])):
            for part in range(2):
                sends, copy = tree_copy(level, number, part, OWN)

                @pl.when(sends)
                def _():
                    copy.wait_send()

    for which in range(2):
        for chunk in range(CASTS):
            for child in range(4):

                @pl.when(children[child][0])
                def _():
                    cast_copy(which, chunk, child).wait_send()

    for chunk in range(CASTS):
        part_copy(chunk).wait_send()

    @pl.when(core == 1)
    def _():
        extra_copy.wait_send()

    @pl.when(core == 0)
    def _():
        for chunk in range(CHUNKS):
            hand_copy(chunk).wait_send()

        @pl.when(y < chips - 1)
        def _():
            for chunk in range(CHUNKS):
                chain_copy(chunk).wait_send()

    store_down.wait()
    store_bounced.wait()
    store_mark.wait()


def layers(doublings, slabs, incident):
    order = slabs.shape[-1]
    rows = incident.shape[1]
    depth = lax.axis_size("depth")
    block = jax.ShapeDtypeStruct(incident.shape, F32)
    matrix = pltpu.VMEM((order, order), F32)
    halves = pltpu.VMEM((2, order, order), BF16)
    fields = pltpu.VMEM((rows, order), F32)
    dma = pltpu.SemaphoreType.DMA
    return pl.pallas_call(
        functools.partial(kernel, doublings),
        out_shape=(block, block, jax.ShapeDtypeStruct((8, 128), F32)),
        in_specs=[pl.BlockSpec(memory_space=pl.ANY)] * 2,
        out_specs=[pl.BlockSpec(memory_space=pl.ANY)] * 3,
        scratch_shapes=[
            pltpu.VMEM((BLOCKS, order, order), F32),
            matrix, matrix, matrix,
            fields, fields, fields, fields, fields, fields,
            halves, halves,
            dma((5,)), dma((3,)),
            dma((LEVELS, 2, 2)), dma((LEVELS, 3, 2)),
            dma((2, CASTS, 4)), dma((2, CASTS)),
            dma((CHUNKS,)), dma((CHUNKS,)),
            dma((CHUNKS,)), dma((CHUNKS,)),
            dma, dma,
            dma((CASTS,)), dma((CASTS,)),
            pltpu.VMEM((depth, 8, 128), F32), pltpu.VMEM((8, 128), F32),
            dma((depth,)), dma((depth,)),
        ],
        compiler_params=pltpu.CompilerParams(
            collective_id=int(doublings > DOUBLINGS), has_side_effects=True, vmem_limit_bytes=60 * 2**20
        ),
        name=f"layers{doublings}",
    )(slabs, incident)


def shards(slabs, incident):
    down, bounced, settled = layers(DOUBLINGS, slabs, incident)
    return lax.cond(
        settled[0, 0] == 0.0,
        lambda: (down, bounced),
        lambda: tuple(layers(MORE_DOUBLINGS, slabs, incident)[:2]),
    )


def solution(mesh):
    placed = (P("depth", "slab", None, None, None), P("depth", "slab", None))
    return jax.shard_map(
        shards,
        mesh=mesh,
        in_specs=placed,
        out_specs=(P("depth", "slab", None), P("depth", "slab", None)),
        check_vma=False,
    )
```

```python
import functools

import jax
import jax.numpy as jnp
from jax import lax
from jax.experimental import pallas as pl
from jax.experimental.pallas import tpu as pltpu
from jax.sharding import PartitionSpec as P

F32 = jnp.float32
BF16 = jnp.bfloat16
MESH = pl.DeviceIdType.MESH
DOUBLINGS = 3
MORE_DOUBLINGS = 24
REMAINDER = 1e-5
CHUNKS = 8
CASTS = 8
ROOT_Z = 1
EARLY = 2
LEVELS = 5
OWN = 8 * LEVELS
PARTNER = OWN + 4
BLOCKS = OWN + 5
FINAL_R = 8 * (LEVELS - 1) + 6
FINAL_T = FINAL_R + 1


def split(value):
    high = value.astype(BF16)
    return high, (value - high.astype(F32)).astype(BF16)


def dot(left, right):
    return jnp.dot(left, right, preferred_element_type=F32)


def split_dot(left, right):
    return dot(left[0], right[0]) + (dot(left[0], right[1]) + dot(left[1], right[0]))


def matmul(left, right):
    return split_dot(split(left), split(right))


def kernel(
    doublings, slabs, incident, down, bounced, settled,
    buf, power, inverse, coupled, field, arrive, leave, handed, handing, extra, pair_t, bounce_t,
    load_sem, store_sem, tree_send, tree_recv, cast_send, cast_recv,
    chain_send, chain_recv, hand_send, hand_recv, extra_send, extra_recv, part_send, part_recv,
    heads, poison, relay_send, relay_recv,
):
    slab = lax.axis_index("slab")
    depth = lax.axis_index("depth")
    x = lax.rem(slab, 4)
    z = lax.div(slab, 4)
    core = lax.rem(depth, 2)
    y = lax.div(depth, 2)
    chips = lax.axis_size("depth") // 2
    order = buf.shape[1]
    rows = field.shape[0] // CHUNKS
    band = order // CASTS

    loads = [
        pltpu.make_async_copy(slabs.at[0, 0, i], buf.at[OWN + i], load_sem.at[i]) for i in range(4)
    ]
    loads.append(pltpu.make_async_copy(incident.at[0], field, load_sem.at[4]))
    for load in loads:
        load.start()

    def at(px, pz):
        return lax.rem(pz + 16, 8) * 4 + lax.rem(px + 8, 4)

    rt_x = 1 - core
    qu_x = 2 + core
    root_z = ROOT_Z

    def slot(level, pair, part):
        return level * 8 + pair * 2 + part

    outer = (x == 0) | (x == 3)
    on_rt = x == rt_x
    on_qu = x == qu_x
    z2 = lax.rem(z, 2)
    z4 = lax.rem(z, 4)
    mirror = at(3 - x, z)
    crossing2 = (on_qu & (z2 == 0)) | (on_rt & (z2 == 1))
    merged2 = (on_rt & (z2 == 0)) | (on_qu & (z2 == 1))
    inner3 = (on_qu & (z4 == 1)) | (on_rt & (z4 == 2))
    ahead3 = jnp.where(z4 < 2, 1, -1)
    row = z == root_z
    root = row & (on_rt | on_qu)
    from_qu = on_qu & (z == root_z + 1)
    from_rt = on_rt & (z == root_z + 4)

    barrier = pltpu.get_barrier_semaphore()

    def greet(**target):
        pl.semaphore_signal(barrier, inc=1, device_id=target, device_id_type=MESH)

    for px, pz in ((1, 0), (-1, 0), (2, 0), (0, 1), (0, -1)):
        greet(slab=at(x + px, z + pz))
    greet(depth=depth + 1 - 2 * core)

    @pl.when(y > 0)
    def _():
        greet(depth=depth - 2)

    @pl.when(y < chips - 1)
    def _():
        greet(depth=depth + 2)

    meetings = [
        (from_qu, at(rt_x, root_z)),
        (from_rt, at(rt_x, root_z)),
        (from_rt, at(qu_x, root_z)),
        (root & on_rt, at(qu_x, root_z + 1)),
        (root & on_rt, at(rt_x, root_z + 4)),
        (root & on_qu, at(rt_x, root_z + 4)),
    ]
    for meets, target in meetings:

        @pl.when(meets)
        def _(target=target):
            greet(slab=target)

    met = [y > 0, y < chips - 1] + [meets for meets, _ in meetings]
    pl.semaphore_wait(barrier, 6 + sum(flag.astype(jnp.int32) for flag in met))

    true = x >= 0
    routes = [
        [(true, at(x + 1 - 2 * lax.rem(x, 2), z), 2)],
        [
            (jnp.logical_not(outer), jnp.where(core == 0, mirror, at(x + 2, z)), 2),
            (outer == (core == 0), at(x + 1 - 2 * lax.rem(x, 2), z), core),
        ],
        [
            (crossing2, mirror, 1),
            (crossing2, at(x, z + 1 - 2 * z2), 2),
        ],
        [
            (inner3, mirror, 1),
            (merged2, at(x, z + ahead3), jnp.where(inner3, 2, 0)),
        ],
        [
            (from_qu | from_rt, at(rt_x, root_z), jnp.where(on_qu, 1, 2)),
            (from_qu | from_rt | (root & on_rt), at(qu_x, root_z), jnp.where(on_qu, 1, jnp.where(row, 0, 2))),
        ],
    ]
    computes = [
        true,
        on_rt | on_qu,
        merged2,
        (on_rt & (z4 == 1)) | (on_qu & (z4 == 2)),
        root,
    ]
    local = [3, 1 - core, 0, 3, jnp.where(on_rt, 0, 3)]

    def tree_copy(level, number, part, source):
        sends, target, pair = routes[level][number]
        return sends, pltpu.make_async_remote_copy(
            src_ref=buf.at[source],
            dst_ref=buf.at[slot(level, pair, part)],
            send_sem=tree_send.at[level, number, part],
            recv_sem=tree_recv.at[level, pair, part],
            device_id={"slab": target},
            device_id_type=MESH,
        )

    def send_part(level, part, source):
        for number in range(len(routes[level])):
            sends, copy = tree_copy(level, number, part, source)

            @pl.when(sends)
            def _():
                copy.start()

    def await_part(level, pair, part):
        pltpu.make_async_remote_copy(
            src_ref=buf.at[slot(level, pair, part)],
            dst_ref=buf.at[slot(level, pair, part)],
            send_sem=tree_send.at[level, 0, part],
            recv_sem=tree_recv.at[level, pair, part],
            device_id={"slab": slab},
            device_id_type=MESH,
        ).wait_recv()

    for load in loads[:4]:
        load.wait()
    odd = lax.rem(x, 2) == 1
    first_pair = jnp.where(odd, OWN, OWN + 2)
    add_pair = jnp.where(odd, OWN + 2, OWN)
    send_part(0, 0, first_pair)
    send_part(0, 1, first_pair + 1)

    def operand(level, pair, part):
        if level == 0:
            if pair == 2:
                return slot(0, 2, part)
            return (add_pair if pair == 0 else first_pair) + part
        own = slot(level - 1, 3, part)
        known = local[level]
        if isinstance(known, int):
            return own if known == pair else slot(level, pair, part)
        return jnp.where(known == pair, own, slot(level, pair, part))

    def arrived(level, pair, part):
        if level == 0:
            if pair == 2:
                await_part(0, 2, part)
            return
        known = local[level]
        if isinstance(known, int):
            if known != pair:
                await_part(level, pair, part)
            return

        @pl.when(known != pair)
        def _():
            await_part(level, pair, part)

    def merge(level):
        arrived(level, 1, 0)
        arrived(level, 2, 0)
        near = buf[operand(level, 1, 0)]
        far = split(buf[operand(level, 2, 0)])
        system = split_dot(split(near), far)
        ones = lax.broadcasted_iota(jnp.int32, (order, order), 0) == lax.broadcasted_iota(jnp.int32, (order, order), 1)
        inverse[...] = system + jnp.where(ones, 1.0, 0.0)
        power[...] = system

        def double(halves):
            squared = split_dot(halves, halves)
            power[...] = squared
            whole = inverse[...]
            inverse[...] = whole + split_dot(split(squared), split(whole))

        if doublings <= DOUBLINGS:
            for _ in range(doublings - 1):
                double(split(power[...]))
            last = jnp.square(power[...]).reshape(order // 8, 8, order // 128, 128)
            poison[...] = jnp.where(jnp.sum(last, axis=(0, 2)) < REMAINDER / 1024, 0.0, jnp.nan)
        else:

            def step(_, carry):
                double(split(power[...]))
                return carry

            lax.fori_loop(0, doublings - 1, step, 0)
        solved = split(inverse[...])
        coupled[...] = split_dot(far, solved)
        arrived(level, 0, 1)
        right = split(buf[operand(level, 0, 1)])
        through = split_dot(solved, right)
        turned = split_dot(split(coupled[...]), right)
        head = (pl.ds(0, 8), pl.ds(0, 128))

        def finish(part, value):
            place = slot(level, 3, part)
            buf[place] = value
            if doublings <= DOUBLINGS:
                buf[(place, *head)] += poison[...]
            if level + 1 < LEVELS:
                send_part(level + 1, part, place)

        def reflection():
            arrived(level, 1, 1)
            arrived(level, 0, 0)
            finish(0, buf[operand(level, 0, 0)] + matmul(buf[operand(level, 1, 1)], turned))

        def transmission():
            arrived(level, 2, 1)
            finish(1, matmul(buf[operand(level, 2, 1)], through))

        if level + 1 < LEVELS:
            reflection()
            transmission()
        else:
            transmission()
            reflection()

    for level in range(LEVELS):

        @pl.when(computes[level])
        def _(level=level):
            merge(level)

    dz = lax.rem(z - root_z + 8, 8)
    on_pair = on_rt | on_qu
    x_line = (core == 1) | row
    z_line = (core == 0) | on_pair
    children = [
        (on_pair & x_line, at(x + 1 - 2 * lax.rem(x, 2), z)),
        (z_line & (dz <= 3), at(x, z + 1)),
        (z_line & ((dz == 0) | (dz >= 6)), at(x, z - 1)),
    ]

    def cast_copy(which, chunk, child):
        place = buf.at[FINAL_R + which, pl.ds(chunk * band, band)]
        return pltpu.make_async_remote_copy(
            src_ref=place,
            dst_ref=place,
            send_sem=cast_send.at[which, chunk, child],
            recv_sem=cast_recv.at[which, chunk],
            device_id={"slab": children[child][1]},
            device_id_type=MESH,
        )

    def part_copy(chunk):
        return pltpu.make_async_remote_copy(
            src_ref=buf.at[FINAL_T, pl.ds(chunk * band, band)],
            dst_ref=buf.at[PARTNER, pl.ds(chunk * band, band)],
            send_sem=part_send.at[chunk],
            recv_sem=part_recv.at[chunk],
            device_id={"depth": depth + 1 - 2 * core},
            device_id_type=MESH,
        )

    def relay_copy(way):
        return pltpu.make_async_remote_copy(
            src_ref=heads.at[way],
            dst_ref=heads.at[2 + way],
            send_sem=relay_send.at[way],
            recv_sem=relay_recv.at[way],
            device_id={"depth": lax.rem(depth + (2 * chips - 2 if way else 2), 2 * chips)},
            device_id_type=MESH,
        )

    first = y == 0
    final = y == chips - 1

    def relay(way):
        head = (pl.ds(0, 8), pl.ds(0, 128))
        start, end = (final, first) if way else (first, final)
        heads[way] = (buf[(FINAL_T, *head)] + buf[(PARTNER, *head)]) * 0.0

        @pl.when(jnp.logical_not(start))
        def _():
            relay_copy(way).wait_recv()
            heads[way] += heads[2 + way]

        @pl.when(jnp.logical_not(end))
        def _():
            relay_copy(way).start()

    def forward(which):
        for chunk in range(CASTS):

            @pl.when(jnp.logical_not(root))
            def _():
                cast_copy(which, chunk, 0).wait_recv()

            for child in range(3):

                @pl.when(children[child][0])
                def _():
                    cast_copy(which, chunk, child).start()

            if which == 1:
                part_copy(chunk).start()

    def keep_split(ref, value):
        ref[0], ref[1] = split(value)

    def kept(ref):
        return ref[0], ref[1]

    def forward_r():
        forward(0)
        keep_split(bounce_t, buf[FINAL_R].T)

    extra_copy = pltpu.make_async_remote_copy(
        src_ref=extra,
        dst_ref=extra,
        send_sem=extra_send,
        recv_sem=extra_recv,
        device_id={"depth": depth + 1 - 2 * core},
        device_id_type=MESH,
    )

    def chain_copy(chunk):
        return pltpu.make_async_remote_copy(
            src_ref=leave.at[pl.ds(chunk * rows, rows)],
            dst_ref=arrive.at[pl.ds(chunk * rows, rows)],
            send_sem=chain_send.at[chunk],
            recv_sem=chain_recv.at[chunk],
            device_id={"depth": lax.rem(depth + 2, 2 * chips)},
            device_id_type=MESH,
        )

    def hand_copy(chunk):
        return pltpu.make_async_remote_copy(
            src_ref=field.at[pl.ds(chunk * rows, rows)],
            dst_ref=handed.at[pl.ds(chunk * rows, rows)],
            send_sem=hand_send.at[chunk],
            recv_sem=hand_recv.at[chunk],
            device_id={"depth": depth + 1 - 2 * core},
            device_id_type=MESH,
        )

    forward(1)
    loads[4].wait()

    @pl.when(core == 1)
    def _():
        keep_split(pair_t, buf[FINAL_T].T)
        extra[...] = split_dot(split(field[...]), kept(pair_t))
        extra_copy.start()
        for chunk in range(CASTS):
            part_copy(chunk).wait_recv()
        keep_split(pair_t, buf[PARTNER].T)

        @pl.when(y >= chips // 2)
        def _():
            relay(1)

        forward_r()
        for chunk in range(CHUNKS):
            part = pl.ds(chunk * rows, rows)
            hand_copy(chunk).wait_recv()
            field[part] += split_dot(split(handed[part]), kept(pair_t))

        relay(0)

        @pl.when(y < chips // 2)
        def _():
            relay(1)

    @pl.when(core == 0)
    def _():
        for chunk in range(CASTS):
            part_copy(chunk).wait_recv()
        keep_split(pair_t, matmul(buf[PARTNER], buf[FINAL_T]).T)
        extra_copy.wait_recv()
        extra[...] += split_dot(split(field[...]), kept(pair_t))

        @pl.when(y == 0)
        def _():
            for chunk in range(CHUNKS):
                part = pl.ds(chunk * rows, rows)
                leave[part] = extra[part]
                chain_copy(chunk).start()
                hand_copy(chunk).start()

        @pl.when(y >= chips // 2)
        def _():
            relay(1)

        @pl.when(y > EARLY)
        def _():
            forward_r()

        @pl.when(y > 0)
        def _():
            for chunk in range(CHUNKS):
                part = pl.ds(chunk * rows, rows)
                chain_copy(chunk).wait_recv()

                @pl.when(y < chips - 1)
                def _():
                    leave[part] = extra[part] + split_dot(split(arrive[part]), kept(pair_t))
                    chain_copy(chunk).start()

                field[part] += arrive[part]
                hand_copy(chunk).start()

        relay(0)

        @pl.when(y <= EARLY)
        def _():
            forward_r()

        @pl.when(y < chips // 2)
        def _():
            relay(1)

    store_down = pltpu.make_async_copy(field, down.at[0], store_sem.at[0])
    store_down.start()

    handing[...] = split_dot(split(field[...]), kept(bounce_t))
    store_bounced = pltpu.make_async_copy(handing, bounced.at[0], store_sem.at[1])
    store_bounced.start()

    settled[0, 0] = jnp.sum(heads[0] + heads[1])

    for level in range(LEVELS):
        for number in range(len(routes[level])):
            for part in range(2):
                sends, copy = tree_copy(level, number, part, OWN)

                @pl.when(sends)
                def _():
                    copy.wait_send()

    for which in range(2):
        for chunk in range(CASTS):
            for child in range(3):

                @pl.when(children[child][0])
                def _():
                    cast_copy(which, chunk, child).wait_send()

    for chunk in range(CASTS):
        part_copy(chunk).wait_send()

    @pl.when(core == 1)
    def _():
        extra_copy.wait_send()

    @pl.when(core == 0)
    def _():
        for chunk in range(CHUNKS):
            hand_copy(chunk).wait_send()

        @pl.when(y < chips - 1)
        def _():
            for chunk in range(CHUNKS):
                chain_copy(chunk).wait_send()

    @pl.when(jnp.logical_not(final))
    def _():
        relay_copy(0).wait_send()

    @pl.when(jnp.logical_not(first))
    def _():
        relay_copy(1).wait_send()

    store_down.wait()
    store_bounced.wait()


def layers(doublings, slabs, incident):
    order = slabs.shape[-1]
    rows = incident.shape[1]
    block = jax.ShapeDtypeStruct(incident.shape, F32)
    matrix = pltpu.VMEM((order, order), F32)
    halves = pltpu.VMEM((2, order, order), BF16)
    fields = pltpu.VMEM((rows, order), F32)
    dma = pltpu.SemaphoreType.DMA
    return pl.pallas_call(
        functools.partial(kernel, doublings),
        out_shape=(block, block, jax.ShapeDtypeStruct((1, 1), F32)),
        in_specs=[pl.BlockSpec(memory_space=pl.ANY)] * 2,
        out_specs=[pl.BlockSpec(memory_space=pl.ANY)] * 2 + [pl.BlockSpec(memory_space=pltpu.SMEM)],
        scratch_shapes=[
            pltpu.VMEM((BLOCKS, order, order), F32),
            matrix, matrix, matrix,
            fields, fields, fields, fields, fields, fields,
            halves, halves,
            dma((5,)), dma((2,)),
            dma((LEVELS, 2, 2)), dma((LEVELS, 3, 2)),
            dma((2, CASTS, 3)), dma((2, CASTS)),
            dma((CHUNKS,)), dma((CHUNKS,)),
            dma((CHUNKS,)), dma((CHUNKS,)),
            dma, dma,
            dma((CASTS,)), dma((CASTS,)),
            pltpu.VMEM((4, 8, 128), F32), pltpu.VMEM((8, 128), F32),
            dma((2,)), dma((2,)),
        ],
        compiler_params=pltpu.CompilerParams(
            collective_id=int(doublings > DOUBLINGS), has_side_effects=True, vmem_limit_bytes=60 * 2**20
        ),
        name=f"layers{doublings}",
    )(slabs, incident)


def shards(slabs, incident):
    down, bounced, settled = layers(DOUBLINGS, slabs, incident)
    return lax.cond(
        settled[0, 0] == 0.0,
        lambda: (down, bounced),
        lambda: tuple(layers(MORE_DOUBLINGS, slabs, incident)[:2]),
    )


def solution(mesh):
    placed = (P("depth", "slab", None, None, None), P("depth", "slab", None))
    return jax.shard_map(
        shards,
        mesh=mesh,
        in_specs=placed,
        out_specs=(P("depth", "slab", None), P("depth", "slab", None)),
        check_vma=False,
    )
```

```python
import functools

import jax
import jax.numpy as jnp
from jax import lax
from jax.experimental import pallas as pl
from jax.experimental.pallas import tpu as pltpu
from jax.sharding import PartitionSpec as P

F32 = jnp.float32
BF16 = jnp.bfloat16
MESH = pl.DeviceIdType.MESH
DOUBLINGS = 3
MORE_DOUBLINGS = 24
REMAINDER = 1e-5
CHUNKS = 8
CASTS = 8
ROOT_Z = 1
EARLY = 2
LEVELS = 5
OWN = 8 * LEVELS
PARTNER = OWN + 4
BLOCKS = OWN + 5
TAKEN = 2
KEPT = 0
FINAL_R = 8 * (LEVELS - 1) + 6
FINAL_T = FINAL_R + 1


def split(value):
    high = value.astype(BF16)
    return high, (value - high.astype(F32)).astype(BF16)


def dot(left, right):
    return jnp.dot(left, right, preferred_element_type=F32)


def split_dot(left, right):
    return dot(left[0], right[0]) + (dot(left[0], right[1]) + dot(left[1], right[0]))


def matmul(left, right):
    return split_dot(split(left), split(right))


def kernel(
    doublings, slabs, incident, down, bounced, settled,
    buf, power, inverse, coupled, field, arrive, leave, handed, handing, extra, pair_t, bounce_t,
    load_sem, store_sem, tree_send, tree_recv, cast_send, cast_recv,
    chain_send, chain_recv, hand_send, hand_recv, extra_send, extra_recv, part_send, part_recv,
    heads, poison, relay_send, relay_recv, give_send, give_recv,
):
    slab = lax.axis_index("slab")
    depth = lax.axis_index("depth")
    x = lax.rem(slab, 4)
    z = lax.div(slab, 4)
    core = lax.rem(depth, 2)
    y = lax.div(depth, 2)
    chips = lax.axis_size("depth") // 2
    order = buf.shape[1]
    rows = field.shape[0] // CHUNKS
    band = order // CASTS

    loads = [
        pltpu.make_async_copy(slabs.at[0, 0, i], buf.at[OWN + i], load_sem.at[i]) for i in range(4)
    ]
    loads.append(pltpu.make_async_copy(incident.at[0], field, load_sem.at[4]))
    for load in loads:
        load.start()

    def at(px, pz):
        return lax.rem(pz + 16, 8) * 4 + lax.rem(px + 8, 4)

    rt_x = 1 - core
    qu_x = 2 + core
    root_z = ROOT_Z

    def slot(level, pair, part):
        return level * 8 + pair * 2 + part

    on_rt = x == rt_x
    on_qu = x == qu_x
    z2 = lax.rem(z, 2)
    z4 = lax.rem(z, 4)
    mirror = at(3 - x, z)
    odd = lax.rem(x, 2) == 1
    beside = at(x + 1 - 2 * lax.rem(x, 2), z)
    takes = on_rt | on_qu
    crossing2 = (on_qu & (z2 == 0)) | (on_rt & (z2 == 1))
    merged2 = (on_rt & (z2 == 0)) | (on_qu & (z2 == 1))
    inner3 = (on_qu & (z4 == 1)) | (on_rt & (z4 == 2))
    ahead3 = jnp.where(z4 < 2, 1, -1)
    row = z == root_z
    root = row & on_rt
    from_qu = on_qu & (z == root_z + 1)
    from_rt = on_rt & (z == root_z + 4)

    barrier = pltpu.get_barrier_semaphore()

    def greet(**target):
        pl.semaphore_signal(barrier, inc=1, device_id=target, device_id_type=MESH)

    for px, pz in ((1, 0), (-1, 0), (0, 1), (0, -1)):
        greet(slab=at(x + px, z + pz))
    greet(depth=depth + 1 - 2 * core)

    @pl.when(y > 0)
    def _():
        greet(depth=depth - 2)

    @pl.when(y < chips - 1)
    def _():
        greet(depth=depth + 2)

    meetings = [
        (from_qu, at(rt_x, root_z)),
        (from_rt, at(rt_x, root_z)),
        (root, at(qu_x, root_z + 1)),
        (root, at(rt_x, root_z + 4)),
    ]
    for meets, target in meetings:

        @pl.when(meets)
        def _(target=target):
            greet(slab=target)

    met = [y > 0, y < chips - 1] + [meets for meets, _ in meetings]
    pl.semaphore_wait(barrier, 5 + sum(flag.astype(jnp.int32) for flag in met))

    routes = [
        [],
        [(takes, mirror, 2)],
        [
            (crossing2, mirror, 1),
            (crossing2, at(x, z + 1 - 2 * z2), 2),
        ],
        [
            (inner3, mirror, 1),
            (merged2, at(x, z + ahead3), jnp.where(inner3, 2, 0)),
        ],
        [
            (from_qu | from_rt, at(rt_x, root_z), jnp.where(on_qu, 1, 2)),
        ],
    ]
    computes = [
        takes,
        takes,
        merged2,
        (on_rt & (z4 == 1)) | (on_qu & (z4 == 2)),
        root,
    ]
    local = [3, 3, 0, 3, 0]

    def tree_copy(level, number, part, source):
        sends, target, pair = routes[level][number]
        return sends, pltpu.make_async_remote_copy(
            src_ref=buf.at[source],
            dst_ref=buf.at[slot(level, pair, part)],
            send_sem=tree_send.at[level, number, part],
            recv_sem=tree_recv.at[level, pair, part],
            device_id={"slab": target},
            device_id_type=MESH,
        )

    def send_part(level, part, source):
        for number in range(len(routes[level])):
            sends, copy = tree_copy(level, number, part, source)

            @pl.when(sends)
            def _():
                copy.start()

    def await_part(level, pair, part):
        pltpu.make_async_remote_copy(
            src_ref=buf.at[slot(level, pair, part)],
            dst_ref=buf.at[slot(level, pair, part)],
            send_sem=tree_send.at[level, 0, part],
            recv_sem=tree_recv.at[level, pair, part],
            device_id={"slab": slab},
            device_id_type=MESH,
        ).wait_recv()

    for load in loads[:4]:
        load.wait()
    second = jnp.where(odd == (core == 0), 1, 3)
    blocks = [jnp.where(odd, 0, 2), second, 4 - second, jnp.where(odd, 2, 0)]

    def give_copy(turn):
        return pltpu.make_async_remote_copy(
            src_ref=buf.at[OWN + blocks[turn]],
            dst_ref=buf.at[TAKEN + blocks[turn]],
            send_sem=give_send.at[turn],
            recv_sem=give_recv.at[turn],
            device_id={"slab": beside},
            device_id_type=MESH,
        )

    @pl.when(jnp.logical_not(takes))
    def _():
        for turn in range(4):
            give_copy(turn).start()

    head = (pl.ds(0, 8), pl.ds(0, 128))

    def merge(place, wait, finish, transmission_first=False):
        wait("p1")
        wait("p2")
        near = buf[place["p1"]]
        far = split(buf[place["p2"]])
        system = split_dot(split(near), far)
        ones = lax.broadcasted_iota(jnp.int32, (order, order), 0) == lax.broadcasted_iota(jnp.int32, (order, order), 1)
        inverse[...] = system + jnp.where(ones, 1.0, 0.0)
        power[...] = system

        def double(halves):
            squared = split_dot(halves, halves)
            power[...] = squared
            whole = inverse[...]
            inverse[...] = whole + split_dot(split(squared), split(whole))

        if doublings <= DOUBLINGS:
            for _ in range(doublings - 1):
                double(split(power[...]))
            last = jnp.square(power[...]).reshape(order // 8, 8, order // 128, 128)
            poison[...] = jnp.where(jnp.sum(last, axis=(0, 2)) < REMAINDER / 1024, 0.0, jnp.nan)
        else:

            def step(_, carry):
                double(split(power[...]))
                return carry

            lax.fori_loop(0, doublings - 1, step, 0)
        solved = split(inverse[...])
        coupled[...] = split_dot(far, solved)
        wait("s")
        right = split(buf[place["s"]])
        through = split_dot(solved, right)
        turned = split_dot(split(coupled[...]), right)

        def reflection():
            wait("m1")
            wait("add")
            finish(0, buf[place["add"]] + matmul(buf[place["m1"]], turned))

        def transmission():
            wait("m2")
            finish(1, matmul(buf[place["m2"]], through))

        if transmission_first:
            transmission()
            reflection()
        else:
            reflection()
            transmission()

    def put(place, value):
        buf[place] = value
        if doublings <= DOUBLINGS:
            buf[(place, *head)] += poison[...]

    upper = jnp.where(odd, TAKEN, OWN)
    lower = jnp.where(odd, OWN, TAKEN)

    def sides(is_qu):
        return {
            "p1": jnp.where(is_qu, lower, upper + 2),
            "p2": jnp.where(is_qu, upper + 2, lower),
            "s": jnp.where(is_qu, lower + 3, upper + 1),
            "add": jnp.where(is_qu, lower + 2, upper),
            "m1": jnp.where(is_qu, lower + 1, upper + 3),
            "m2": jnp.where(is_qu, upper + 3, lower + 1),
        }

    def given(turns):
        def wait(name):
            if name in turns:
                give_copy(turns[name]).wait_recv()

        return wait

    def finish_sent(part, value):
        put(slot(0, 3, part), value)
        send_part(1, part, slot(0, 3, part))

    def finish_kept(part, value):
        put(KEPT + part, value)

    @pl.when(takes & (core == 0))
    def _():
        merge(sides(x < 2), given({"p1": 0, "m2": 1}), finish_sent)
        merge(sides(x >= 2), given({"s": 2, "add": 3}), finish_kept)

    @pl.when(takes & (core == 1))
    def _():
        merge(sides(x < 2), given({"p1": 0, "s": 1, "m1": 2, "add": 3}), finish_sent, transmission_first=True)
        merge(sides(x >= 2), given({}), finish_kept)

    names = {"add": (0, 0), "s": (0, 1), "p1": (1, 0), "m1": (1, 1), "p2": (2, 0), "m2": (2, 1)}

    def merge_level(level):
        def operand(pair, part):
            if level == 1:
                return [KEPT + part, slot(0, 3, part), slot(1, 2, part)][pair]
            return slot(level - 1, 3, part) if local[level] == pair else slot(level, pair, part)

        def wait(name):
            pair, part = names[name]
            if pair == 2 if level == 1 else pair != local[level]:
                await_part(level, pair, part)

        def finish(part, value):
            put(slot(level, 3, part), value)
            if level + 1 < LEVELS:
                send_part(level + 1, part, slot(level, 3, part))

        place = {name: operand(*key) for name, key in names.items()}
        merge(place, wait, finish, transmission_first=level + 1 == LEVELS)

    for level in range(1, LEVELS):

        @pl.when(computes[level])
        def _(level=level):
            merge_level(level)

    dx = lax.rem(x - rt_x + 4, 4)
    dz = lax.rem(z - root_z + 8, 8)
    x_first = core == 0
    x_line = jnp.logical_not(x_first) | row
    z_line = x_first | (dx == 0)
    children = [
        (x_line & ((dx == 0) | (x_first & (dx == 1))), at(x + 1, z)),
        (x_line & ((dx == 0) | (jnp.logical_not(x_first) & (dx == 3))), at(x - 1, z)),
        (z_line & (dz <= 3), at(x, z + 1)),
        (z_line & ((dz == 0) | (dz >= 6)), at(x, z - 1)),
    ]

    def cast_copy(which, chunk, child):
        place = buf.at[FINAL_R + which, pl.ds(chunk * band, band)]
        return pltpu.make_async_remote_copy(
            src_ref=place,
            dst_ref=place,
            send_sem=cast_send.at[which, chunk, child],
            recv_sem=cast_recv.at[which, chunk],
            device_id={"slab": children[child][1]},
            device_id_type=MESH,
        )

    def part_copy(chunk):
        return pltpu.make_async_remote_copy(
            src_ref=buf.at[FINAL_T, pl.ds(chunk * band, band)],
            dst_ref=buf.at[PARTNER, pl.ds(chunk * band, band)],
            send_sem=part_send.at[chunk],
            recv_sem=part_recv.at[chunk],
            device_id={"depth": depth + 1 - 2 * core},
            device_id_type=MESH,
        )

    def relay_copy(way):
        return pltpu.make_async_remote_copy(
            src_ref=heads.at[way],
            dst_ref=heads.at[2 + way],
            send_sem=relay_send.at[way],
            recv_sem=relay_recv.at[way],
            device_id={"depth": lax.rem(depth + (2 * chips - 2 if way else 2), 2 * chips)},
            device_id_type=MESH,
        )

    first = y == 0
    final = y == chips - 1

    def relay(way):
        head = (pl.ds(0, 8), pl.ds(0, 128))
        start, end = (final, first) if way else (first, final)
        heads[way] = (buf[(FINAL_T, *head)] + buf[(PARTNER, *head)]) * 0.0

        @pl.when(jnp.logical_not(start))
        def _():
            relay_copy(way).wait_recv()
            heads[way] += heads[2 + way]

        @pl.when(jnp.logical_not(end))
        def _():
            relay_copy(way).start()

    def forward(which):
        for chunk in range(CASTS):

            @pl.when(jnp.logical_not(root))
            def _():
                cast_copy(which, chunk, 0).wait_recv()

            for child in range(4):

                @pl.when(children[child][0])
                def _():
                    cast_copy(which, chunk, child).start()

            if which == 1:
                part_copy(chunk).start()

    def keep_split(ref, value):
        ref[0], ref[1] = split(value)

    def kept(ref):
        return ref[0], ref[1]

    def forward_r():
        forward(0)
        keep_split(bounce_t, buf[FINAL_R].T)

    extra_copy = pltpu.make_async_remote_copy(
        src_ref=extra,
        dst_ref=extra,
        send_sem=extra_send,
        recv_sem=extra_recv,
        device_id={"depth": depth + 1 - 2 * core},
        device_id_type=MESH,
    )

    def chain_copy(chunk):
        return pltpu.make_async_remote_copy(
            src_ref=leave.at[pl.ds(chunk * rows, rows)],
            dst_ref=arrive.at[pl.ds(chunk * rows, rows)],
            send_sem=chain_send.at[chunk],
            recv_sem=chain_recv.at[chunk],
            device_id={"depth": lax.rem(depth + 2, 2 * chips)},
            device_id_type=MESH,
        )

    def hand_copy(chunk):
        return pltpu.make_async_remote_copy(
            src_ref=field.at[pl.ds(chunk * rows, rows)],
            dst_ref=handed.at[pl.ds(chunk * rows, rows)],
            send_sem=hand_send.at[chunk],
            recv_sem=hand_recv.at[chunk],
            device_id={"depth": depth + 1 - 2 * core},
            device_id_type=MESH,
        )

    forward(1)
    loads[4].wait()

    @pl.when(core == 1)
    def _():
        keep_split(pair_t, buf[FINAL_T].T)
        extra[...] = split_dot(split(field[...]), kept(pair_t))
        extra_copy.start()
        for chunk in range(CASTS):
            part_copy(chunk).wait_recv()
        keep_split(pair_t, buf[PARTNER].T)

        @pl.when(y >= chips // 2)
        def _():
            relay(1)

        forward_r()
        for chunk in range(CHUNKS):
            part = pl.ds(chunk * rows, rows)
            hand_copy(chunk).wait_recv()
            field[part] += split_dot(split(handed[part]), kept(pair_t))

        relay(0)

        @pl.when(y < chips // 2)
        def _():
            relay(1)

    @pl.when(core == 0)
    def _():
        for chunk in range(CASTS):
            part_copy(chunk).wait_recv()
        keep_split(pair_t, matmul(buf[PARTNER], buf[FINAL_T]).T)
        extra_copy.wait_recv()
        extra[...] += split_dot(split(field[...]), kept(pair_t))

        @pl.when(y == 0)
        def _():
            for chunk in range(CHUNKS):
                part = pl.ds(chunk * rows, rows)
                leave[part] = extra[part]
                chain_copy(chunk).start()
                hand_copy(chunk).start()

        @pl.when(y >= chips // 2)
        def _():
            relay(1)

        @pl.when(y > EARLY)
        def _():
            forward_r()

        @pl.when(y > 0)
        def _():
            for chunk in range(CHUNKS):
                part = pl.ds(chunk * rows, rows)
                chain_copy(chunk).wait_recv()

                @pl.when(y < chips - 1)
                def _():
                    leave[part] = extra[part] + split_dot(split(arrive[part]), kept(pair_t))
                    chain_copy(chunk).start()

                field[part] += arrive[part]
                hand_copy(chunk).start()

        relay(0)

        @pl.when(y <= EARLY)
        def _():
            forward_r()

        @pl.when(y < chips // 2)
        def _():
            relay(1)

    store_down = pltpu.make_async_copy(field, down.at[0], store_sem.at[0])
    store_down.start()

    handing[...] = split_dot(split(field[...]), kept(bounce_t))
    store_bounced = pltpu.make_async_copy(handing, bounced.at[0], store_sem.at[1])
    store_bounced.start()

    settled[0, 0] = jnp.sum(heads[0] + heads[1])

    @pl.when(jnp.logical_not(takes))
    def _():
        for turn in range(4):
            give_copy(turn).wait_send()

    for level in range(LEVELS):
        for number in range(len(routes[level])):
            for part in range(2):
                sends, copy = tree_copy(level, number, part, OWN)

                @pl.when(sends)
                def _():
                    copy.wait_send()

    for which in range(2):
        for chunk in range(CASTS):
            for child in range(4):

                @pl.when(children[child][0])
                def _():
                    cast_copy(which, chunk, child).wait_send()

    for chunk in range(CASTS):
        part_copy(chunk).wait_send()

    @pl.when(core == 1)
    def _():
        extra_copy.wait_send()

    @pl.when(core == 0)
    def _():
        for chunk in range(CHUNKS):
            hand_copy(chunk).wait_send()

        @pl.when(y < chips - 1)
        def _():
            for chunk in range(CHUNKS):
                chain_copy(chunk).wait_send()

    @pl.when(jnp.logical_not(final))
    def _():
        relay_copy(0).wait_send()

    @pl.when(jnp.logical_not(first))
    def _():
        relay_copy(1).wait_send()

    store_down.wait()
    store_bounced.wait()


def layers(doublings, slabs, incident):
    order = slabs.shape[-1]
    rows = incident.shape[1]
    block = jax.ShapeDtypeStruct(incident.shape, F32)
    matrix = pltpu.VMEM((order, order), F32)
    halves = pltpu.VMEM((2, order, order), BF16)
    fields = pltpu.VMEM((rows, order), F32)
    dma = pltpu.SemaphoreType.DMA
    return pl.pallas_call(
        functools.partial(kernel, doublings),
        out_shape=(block, block, jax.ShapeDtypeStruct((1, 1), F32)),
        in_specs=[pl.BlockSpec(memory_space=pl.ANY)] * 2,
        out_specs=[pl.BlockSpec(memory_space=pl.ANY)] * 2 + [pl.BlockSpec(memory_space=pltpu.SMEM)],
        scratch_shapes=[
            pltpu.VMEM((BLOCKS, order, order), F32),
            matrix, matrix, matrix,
            fields, fields, fields, fields, fields, fields,
            halves, halves,
            dma((5,)), dma((2,)),
            dma((LEVELS, 2, 2)), dma((LEVELS, 3, 2)),
            dma((2, CASTS, 4)), dma((2, CASTS)),
            dma((CHUNKS,)), dma((CHUNKS,)),
            dma((CHUNKS,)), dma((CHUNKS,)),
            dma, dma,
            dma((CASTS,)), dma((CASTS,)),
            pltpu.VMEM((4, 8, 128), F32), pltpu.VMEM((8, 128), F32),
            dma((2,)), dma((2,)),
            dma((4,)), dma((4,)),
        ],
        compiler_params=pltpu.CompilerParams(
            collective_id=int(doublings > DOUBLINGS), has_side_effects=True, vmem_limit_bytes=60 * 2**20
        ),
        name=f"layers{doublings}",
    )(slabs, incident)


def shards(slabs, incident):
    down, bounced, settled = layers(DOUBLINGS, slabs, incident)
    return lax.cond(
        settled[0, 0] == 0.0,
        lambda: (down, bounced),
        lambda: tuple(layers(MORE_DOUBLINGS, slabs, incident)[:2]),
    )


def solution(mesh):
    placed = (P("depth", "slab", None, None, None), P("depth", "slab", None))
    return jax.shard_map(
        shards,
        mesh=mesh,
        in_specs=placed,
        out_specs=(P("depth", "slab", None), P("depth", "slab", None)),
        check_vma=False,
    )
```

```python
import functools

import jax
import jax.numpy as jnp
from jax import lax
from jax.experimental import pallas as pl
from jax.experimental.pallas import tpu as pltpu
from jax.sharding import PartitionSpec as P

F32 = jnp.float32
BF16 = jnp.bfloat16
MESH = pl.DeviceIdType.MESH
DOUBLINGS = 3
MORE_DOUBLINGS = 24
REMAINDER = 1e-5
CHUNKS = 8
CASTS = 8
ROOT_Z = 1
EARLY = 3
FIRST_SKIP = 3
LEVELS = 5
OWN = 8 * LEVELS
PARTNER = OWN + 4
PRODUCT = OWN + 5
NEXT_PRODUCT = OWN + 6
BLOCKS = OWN + 7
TAKEN = 2
KEPT = 0
FINAL_R = 8 * (LEVELS - 1) + 6
FINAL_T = FINAL_R + 1


def split(value):
    high = value.astype(BF16)
    return high, (value - high.astype(F32)).astype(BF16)


def dot(left, right):
    return jnp.dot(left, right, preferred_element_type=F32)


def split_dot(left, right):
    return dot(left[0], right[0]) + (dot(left[0], right[1]) + dot(left[1], right[0]))


def matmul(left, right):
    return split_dot(split(left), split(right))


def kernel(
    doublings, slabs, incident, down, bounced, settled,
    buf, power, inverse, coupled, field, arrive, leave, handed, handing, extra, leap, ahead, pair_t, bounce_t, skip_t,
    load_sem, store_sem, tree_send, tree_recv, cast_send, cast_recv,
    chain_send, chain_recv, hand_send, hand_recv, extra_send, extra_recv, part_send, part_recv,
    heads, poison, relay_send, relay_recv, give_send, give_recv,
    skip_send, back_send, back_recv,
):
    slab = lax.axis_index("slab")
    depth = lax.axis_index("depth")
    x = lax.rem(slab, 4)
    z = lax.div(slab, 4)
    core = lax.rem(depth, 2)
    y = lax.div(depth, 2)
    chips = lax.axis_size("depth") // 2
    order = buf.shape[1]
    rows = field.shape[0] // CHUNKS
    band = order // CASTS

    loads = [
        pltpu.make_async_copy(slabs.at[0, 0, i], buf.at[OWN + i], load_sem.at[i]) for i in range(4)
    ]
    loads.append(pltpu.make_async_copy(incident.at[0], field, load_sem.at[4]))
    for load in loads:
        load.start()

    def at(px, pz):
        return lax.rem(pz + 16, 8) * 4 + lax.rem(px + 8, 4)

    rt_x = 1 - core
    qu_x = 2 + core
    root_z = ROOT_Z

    def slot(level, pair, part):
        return level * 8 + pair * 2 + part

    on_rt = x == rt_x
    on_qu = x == qu_x
    z2 = lax.rem(z, 2)
    z4 = lax.rem(z, 4)
    mirror = at(3 - x, z)
    odd = lax.rem(x, 2) == 1
    beside = at(x + 1 - 2 * lax.rem(x, 2), z)
    takes = on_rt | on_qu
    crossing2 = (on_qu & (z2 == 0)) | (on_rt & (z2 == 1))
    merged2 = (on_rt & (z2 == 0)) | (on_qu & (z2 == 1))
    inner3 = (on_qu & (z4 == 1)) | (on_rt & (z4 == 2))
    ahead3 = jnp.where(z4 < 2, 1, -1)
    row = lax.rem(z, 4) == root_z
    root = row & on_rt
    near_root = at(rt_x, root_z)
    far_root = at(rt_x, root_z + 4)
    from_qu = on_qu & (z == root_z + 1)
    is_near = root & (z == root_z)
    is_far = root & (z == root_z + 4)

    skips = (core == 0) & (y >= FIRST_SKIP) & (lax.rem(y - FIRST_SKIP, 2) == 0) & (y < chips - 2)
    skipped = (core == 0) & (y > FIRST_SKIP) & (lax.rem(y - FIRST_SKIP, 2) == 1) & (y < chips - 1)
    doubles = skips
    doubled = (core == 0) & (y >= FIRST_SKIP + 2) & (lax.rem(y - FIRST_SKIP, 2) == 0)

    barrier = pltpu.get_barrier_semaphore()

    def greet(**target):
        pl.semaphore_signal(barrier, inc=1, device_id=target, device_id_type=MESH)

    for px, pz in ((1, 0), (-1, 0), (0, 1), (0, -1)):
        greet(slab=at(x + px, z + pz))
    greet(depth=depth + 1 - 2 * core)

    @pl.when(y > 0)
    def _():
        greet(depth=depth - 2)

    @pl.when(y < chips - 1)
    def _():
        greet(depth=depth + 2)

    meetings = [
        (from_qu, near_root),
        (from_qu, far_root),
        (root, at(qu_x, root_z + 1)),
        (is_near, far_root),
        (is_far, near_root),
        (doubles, None),
        (doubled, None),
    ]
    for meets, target in meetings:

        @pl.when(meets)
        def _(target=target, meets=meets):
            if target is not None:
                greet(slab=target)
            else:
                greet(depth=lax.rem(depth + (4 if meets is doubles else 2 * chips - 4), 2 * chips))

    met = [y > 0, y < chips - 1] + [meets for meets, _ in meetings]
    pl.semaphore_wait(barrier, 5 + sum(flag.astype(jnp.int32) for flag in met))

    routes = [
        [],
        [(takes, mirror, 2)],
        [
            (crossing2, mirror, 1),
            (crossing2, at(x, z + 1 - 2 * z2), 2),
        ],
        [
            (inner3, mirror, 1),
            (merged2, at(x, z + ahead3), jnp.where(inner3, 2, 0)),
        ],
        [
            (from_qu | is_far, near_root, jnp.where(on_qu, 1, 2)),
            (from_qu | is_near, far_root, jnp.where(on_qu, 1, 0)),
        ],
    ]
    computes = [
        takes,
        takes,
        merged2,
        (on_rt & (z4 == 1)) | (on_qu & (z4 == 2)),
        root,
    ]
    local = [3, 3, 0, 3, None]

    def tree_copy(level, number, part, source):
        sends, target, pair = routes[level][number]
        return sends, pltpu.make_async_remote_copy(
            src_ref=buf.at[source],
            dst_ref=buf.at[slot(level, pair, part)],
            send_sem=tree_send.at[level, number, part],
            recv_sem=tree_recv.at[level, pair, part],
            device_id={"slab": target},
            device_id_type=MESH,
        )

    def send_part(level, part, source):
        for number in range(len(routes[level])):
            sends, copy = tree_copy(level, number, part, source)

            @pl.when(sends)
            def _():
                copy.start()

    def await_part(level, pair, part):
        pltpu.make_async_remote_copy(
            src_ref=buf.at[slot(level, pair, part)],
            dst_ref=buf.at[slot(level, pair, part)],
            send_sem=tree_send.at[level, 0, part],
            recv_sem=tree_recv.at[level, pair, part],
            device_id={"slab": slab},
            device_id_type=MESH,
        ).wait_recv()

    for load in loads[:4]:
        load.wait()
    second = jnp.where(odd == (core == 0), 1, 3)
    blocks = [jnp.where(odd, 0, 2), second, 4 - second, jnp.where(odd, 2, 0)]

    def give_copy(turn):
        return pltpu.make_async_remote_copy(
            src_ref=buf.at[OWN + blocks[turn]],
            dst_ref=buf.at[TAKEN + blocks[turn]],
            send_sem=give_send.at[turn],
            recv_sem=give_recv.at[turn],
            device_id={"slab": beside},
            device_id_type=MESH,
        )

    @pl.when(jnp.logical_not(takes))
    def _():
        for turn in range(4):
            give_copy(turn).start()

    head = (pl.ds(0, 8), pl.ds(0, 128))

    def merge(place, wait, finish, transmission_first=False):
        wait("p1")
        wait("p2")
        near = buf[place["p1"]]
        far = split(buf[place["p2"]])
        system = split_dot(split(near), far)
        ones = lax.broadcasted_iota(jnp.int32, (order, order), 0) == lax.broadcasted_iota(jnp.int32, (order, order), 1)
        inverse[...] = system + jnp.where(ones, 1.0, 0.0)
        power[...] = system

        def double(halves):
            squared = split_dot(halves, halves)
            power[...] = squared
            whole = inverse[...]
            inverse[...] = whole + split_dot(split(squared), split(whole))

        if doublings <= DOUBLINGS:
            for _ in range(doublings - 1):
                double(split(power[...]))
            last = jnp.square(power[...]).reshape(order // 8, 8, order // 128, 128)
            poison[...] = jnp.where(jnp.sum(last, axis=(0, 2)) < REMAINDER / 1024, 0.0, jnp.nan)
        else:

            def step(_, carry):
                double(split(power[...]))
                return carry

            lax.fori_loop(0, doublings - 1, step, 0)
        solved = split(inverse[...])
        coupled[...] = split_dot(far, solved)
        wait("s")
        right = split(buf[place["s"]])
        through = split_dot(solved, right)
        turned = split_dot(split(coupled[...]), right)

        def reflection():
            wait("m1")
            wait("add")
            finish(0, buf[place["add"]] + matmul(buf[place["m1"]], turned))

        def transmission():
            wait("m2")
            finish(1, matmul(buf[place["m2"]], through))

        if transmission_first:
            transmission()
            reflection()
        else:
            reflection()
            transmission()

    def put(place, value):
        buf[place] = value
        if doublings <= DOUBLINGS:
            buf[(place, *head)] += poison[...]

    upper = jnp.where(odd, TAKEN, OWN)
    lower = jnp.where(odd, OWN, TAKEN)

    def sides(is_qu):
        return {
            "p1": jnp.where(is_qu, lower, upper + 2),
            "p2": jnp.where(is_qu, upper + 2, lower),
            "s": jnp.where(is_qu, lower + 3, upper + 1),
            "add": jnp.where(is_qu, lower + 2, upper),
            "m1": jnp.where(is_qu, lower + 1, upper + 3),
            "m2": jnp.where(is_qu, upper + 3, lower + 1),
        }

    def given(turns):
        def wait(name):
            if name in turns:
                give_copy(turns[name]).wait_recv()

        return wait

    def finish_sent(part, value):
        put(slot(0, 3, part), value)
        send_part(1, part, slot(0, 3, part))

    def finish_kept(part, value):
        put(KEPT + part, value)

    @pl.when(takes & (core == 0))
    def _():
        merge(sides(x < 2), given({"p1": 0, "m2": 1}), finish_sent)
        merge(sides(x >= 2), given({"s": 2, "add": 3}), finish_kept)

    @pl.when(takes & (core == 1))
    def _():
        merge(sides(x < 2), given({"p1": 0, "s": 1, "m1": 2, "add": 3}), finish_sent, transmission_first=True)
        merge(sides(x >= 2), given({}), finish_kept)

    names = {"add": (0, 0), "s": (0, 1), "p1": (1, 0), "m1": (1, 1), "p2": (2, 0), "m2": (2, 1)}

    def merge_level(level):
        def operand(pair, part):
            if level == 1:
                return [KEPT + part, slot(0, 3, part), slot(1, 2, part)][pair]
            if level == 4:
                keeps = is_near if pair == 0 else is_far
                return slot(level, 1, part) if pair == 1 else jnp.where(keeps, slot(3, 3, part), slot(level, pair, part))
            return slot(level - 1, 3, part) if local[level] == pair else slot(level, pair, part)

        def wait(name):
            pair, part = names[name]
            if level == 4 and pair != 1:

                @pl.when(is_far if pair == 0 else is_near)
                def _():
                    await_part(level, pair, part)

                return
            if pair == 2 if level == 1 else pair != local[level]:
                await_part(level, pair, part)

        def finish(part, value):
            put(slot(level, 3, part), value)
            if level + 1 < LEVELS:
                send_part(level + 1, part, slot(level, 3, part))

        place = {name: operand(*key) for name, key in names.items()}
        merge(place, wait, finish, transmission_first=level + 1 == LEVELS)

    for level in range(1, LEVELS):

        @pl.when(computes[level])
        def _(level=level):
            merge_level(level)

    dx = lax.rem(x - rt_x + 4, 4)
    dz = lax.rem(z - root_z + 4, 4)
    x_first = core == 0
    x_line = jnp.logical_not(x_first) | row
    z_line = x_first | (dx == 0)
    children = [
        (x_line & ((dx == 0) | (x_first & (dx == 1))), at(x + 1, z)),
        (x_line & ((dx == 0) | (jnp.logical_not(x_first) & (dx == 3))), at(x - 1, z)),
        (z_line & (dz <= 1), at(x, z + 1)),
        (z_line & (dz == 0), at(x, z - 1)),
    ]

    def cast_copy(which, chunk, child):
        place = buf.at[FINAL_R + which, pl.ds(chunk * band, band)]
        return pltpu.make_async_remote_copy(
            src_ref=place,
            dst_ref=place,
            send_sem=cast_send.at[which, chunk, child],
            recv_sem=cast_recv.at[which, chunk],
            device_id={"slab": children[child][1]},
            device_id_type=MESH,
        )

    def part_copy(chunk):
        return pltpu.make_async_remote_copy(
            src_ref=buf.at[FINAL_T, pl.ds(chunk * band, band)],
            dst_ref=buf.at[PARTNER, pl.ds(chunk * band, band)],
            send_sem=part_send.at[chunk],
            recv_sem=part_recv.at[chunk],
            device_id={"depth": depth + 1 - 2 * core},
            device_id_type=MESH,
        )

    def relay_copy(way):
        return pltpu.make_async_remote_copy(
            src_ref=heads.at[way],
            dst_ref=heads.at[2 + way],
            send_sem=relay_send.at[way],
            recv_sem=relay_recv.at[way],
            device_id={"depth": lax.rem(depth + (2 * chips - 2 if way else 2), 2 * chips)},
            device_id_type=MESH,
        )

    first = y == 0
    final = y == chips - 1

    def relay(way):
        head = (pl.ds(0, 8), pl.ds(0, 128))
        start, end = (final, first) if way else (first, final)
        heads[way] = (buf[(FINAL_T, *head)] + buf[(PARTNER, *head)]) * 0.0

        @pl.when(jnp.logical_not(start))
        def _():
            relay_copy(way).wait_recv()
            heads[way] += heads[2 + way]

        @pl.when(jnp.logical_not(end))
        def _():
            relay_copy(way).start()

    def forward(which):
        for chunk in range(CASTS):

            @pl.when(jnp.logical_not(root))
            def _():
                cast_copy(which, chunk, 0).wait_recv()

            for child in range(4):

                @pl.when(children[child][0])
                def _():
                    cast_copy(which, chunk, child).start()

            if which == 1:
                part_copy(chunk).start()

    def keep_split(ref, value):
        ref[0], ref[1] = split(value)

    def kept(ref):
        return ref[0], ref[1]

    def forward_r():
        forward(0)
        keep_split(bounce_t, buf[FINAL_R].T)

    extra_copy = pltpu.make_async_remote_copy(
        src_ref=extra,
        dst_ref=extra,
        send_sem=extra_send,
        recv_sem=extra_recv,
        device_id={"depth": depth + 1 - 2 * core},
        device_id_type=MESH,
    )

    def chain_copy(chunk):
        return pltpu.make_async_remote_copy(
            src_ref=leave.at[pl.ds(chunk * rows, rows)],
            dst_ref=arrive.at[pl.ds(chunk * rows, rows)],
            send_sem=chain_send.at[chunk],
            recv_sem=chain_recv.at[chunk],
            device_id={"depth": lax.rem(depth + 2, 2 * chips)},
            device_id_type=MESH,
        )

    def skip_copy(chunk):
        return pltpu.make_async_remote_copy(
            src_ref=leap.at[pl.ds(chunk * rows, rows)],
            dst_ref=arrive.at[pl.ds(chunk * rows, rows)],
            send_sem=skip_send.at[chunk],
            recv_sem=chain_recv.at[chunk],
            device_id={"depth": lax.rem(depth + 4, 2 * chips)},
            device_id_type=MESH,
        )

    def back_copy(which):
        source, target = ((buf.at[PRODUCT], buf.at[NEXT_PRODUCT]), (extra, ahead))[which]
        return pltpu.make_async_remote_copy(
            src_ref=source,
            dst_ref=target,
            send_sem=back_send.at[which],
            recv_sem=back_recv.at[which],
            device_id={"depth": lax.rem(depth + 2 * chips - 2, 2 * chips)},
            device_id_type=MESH,
        )

    def hand_copy(chunk):
        return pltpu.make_async_remote_copy(
            src_ref=field.at[pl.ds(chunk * rows, rows)],
            dst_ref=handed.at[pl.ds(chunk * rows, rows)],
            send_sem=hand_send.at[chunk],
            recv_sem=hand_recv.at[chunk],
            device_id={"depth": depth + 1 - 2 * core},
            device_id_type=MESH,
        )

    forward(1)
    loads[4].wait()

    @pl.when(core == 1)
    def _():
        keep_split(pair_t, buf[FINAL_T].T)
        extra[...] = split_dot(split(field[...]), kept(pair_t))
        extra_copy.start()
        for chunk in range(CASTS):
            part_copy(chunk).wait_recv()
        keep_split(pair_t, buf[PARTNER].T)

        @pl.when(y >= chips // 2)
        def _():
            relay(1)

        forward_r()
        for chunk in range(CHUNKS):
            part = pl.ds(chunk * rows, rows)
            hand_copy(chunk).wait_recv()
            field[part] += split_dot(split(handed[part]), kept(pair_t))

        relay(0)

        @pl.when(y < chips // 2)
        def _():
            relay(1)

    @pl.when(core == 0)
    def _():
        for chunk in range(CASTS):
            part_copy(chunk).wait_recv()
        product = matmul(buf[PARTNER], buf[FINAL_T])
        buf[PRODUCT] = product
        keep_split(pair_t, product.T)

        @pl.when(skipped)
        def _():
            back_copy(0).start()

        extra_copy.wait_recv()
        extra[...] += split_dot(split(field[...]), kept(pair_t))

        @pl.when(skipped)
        def _():
            back_copy(1).start()


        @pl.when(y == 0)
        def _():
            for chunk in range(CHUNKS):
                part = pl.ds(chunk * rows, rows)
                leave[part] = extra[part]
                chain_copy(chunk).start()
                hand_copy(chunk).start()

        @pl.when(y >= chips // 2)
        def _():
            relay(1)

        @pl.when(y > EARLY)
        def _():
            forward(0)

        @pl.when(skips)
        def _():
            for which in range(2):
                back_copy(which).wait_recv()
            keep_split(bounce_t, buf[NEXT_PRODUCT].T)
            keep_split(skip_t, split_dot(kept(pair_t), kept(bounce_t)))
            ahead[...] += split_dot(split(extra[...]), kept(bounce_t))

        @pl.when(y > EARLY)
        def _():
            keep_split(bounce_t, buf[FINAL_R].T)

        @pl.when(y > 0)
        def _():
            for chunk in range(CHUNKS):
                part = pl.ds(chunk * rows, rows)
                chain_copy(chunk).wait_recv()

                @pl.when(skips)
                def _():
                    leap[part] = ahead[part] + split_dot(split(arrive[part]), kept(skip_t))
                    skip_copy(chunk).start()

                @pl.when((y < chips - 1) & jnp.logical_not(skipped))
                def _():
                    leave[part] = extra[part] + split_dot(split(arrive[part]), kept(pair_t))
                    chain_copy(chunk).start()

                field[part] += arrive[part]
                hand_copy(chunk).start()

        relay(0)

        @pl.when(y <= EARLY)
        def _():
            forward_r()

        @pl.when(y < chips // 2)
        def _():
            relay(1)

    store_down = pltpu.make_async_copy(field, down.at[0], store_sem.at[0])
    store_down.start()

    handing[...] = split_dot(split(field[...]), kept(bounce_t))
    store_bounced = pltpu.make_async_copy(handing, bounced.at[0], store_sem.at[1])
    store_bounced.start()

    settled[0, 0] = jnp.sum(heads[0] + heads[1])

    @pl.when(jnp.logical_not(takes))
    def _():
        for turn in range(4):
            give_copy(turn).wait_send()

    for level in range(LEVELS):
        for number in range(len(routes[level])):
            for part in range(2):
                sends, copy = tree_copy(level, number, part, OWN)

                @pl.when(sends)
                def _():
                    copy.wait_send()

    for which in range(2):
        for chunk in range(CASTS):
            for child in range(4):

                @pl.when(children[child][0])
                def _():
                    cast_copy(which, chunk, child).wait_send()

    for chunk in range(CASTS):
        part_copy(chunk).wait_send()

    @pl.when(core == 1)
    def _():
        extra_copy.wait_send()

    @pl.when(core == 0)
    def _():
        for chunk in range(CHUNKS):
            hand_copy(chunk).wait_send()

        @pl.when((y < chips - 1) & jnp.logical_not(skipped))
        def _():
            for chunk in range(CHUNKS):
                chain_copy(chunk).wait_send()

        @pl.when(skips)
        def _():
            for chunk in range(CHUNKS):
                skip_copy(chunk).wait_send()

        @pl.when(skipped)
        def _():
            for which in range(2):
                back_copy(which).wait_send()

    @pl.when(jnp.logical_not(final))
    def _():
        relay_copy(0).wait_send()

    @pl.when(jnp.logical_not(first))
    def _():
        relay_copy(1).wait_send()

    store_down.wait()
    store_bounced.wait()


def layers(doublings, slabs, incident):
    order = slabs.shape[-1]
    rows = incident.shape[1]
    block = jax.ShapeDtypeStruct(incident.shape, F32)
    matrix = pltpu.VMEM((order, order), F32)
    halves = pltpu.VMEM((2, order, order), BF16)
    fields = pltpu.VMEM((rows, order), F32)
    dma = pltpu.SemaphoreType.DMA
    return pl.pallas_call(
        functools.partial(kernel, doublings),
        out_shape=(block, block, jax.ShapeDtypeStruct((1, 1), F32)),
        in_specs=[pl.BlockSpec(memory_space=pl.ANY)] * 2,
        out_specs=[pl.BlockSpec(memory_space=pl.ANY)] * 2 + [pl.BlockSpec(memory_space=pltpu.SMEM)],
        scratch_shapes=[
            pltpu.VMEM((BLOCKS, order, order), F32),
            matrix, matrix, matrix,
            fields, fields, fields, fields, fields, fields, fields, fields,
            halves, halves, halves,
            dma((5,)), dma((2,)),
            dma((LEVELS, 2, 2)), dma((LEVELS, 3, 2)),
            dma((2, CASTS, 4)), dma((2, CASTS)),
            dma((CHUNKS,)), dma((CHUNKS,)),
            dma((CHUNKS,)), dma((CHUNKS,)),
            dma, dma,
            dma((CASTS,)), dma((CASTS,)),
            pltpu.VMEM((4, 8, 128), F32), pltpu.VMEM((8, 128), F32),
            dma((2,)), dma((2,)),
            dma((4,)), dma((4,)),
            dma((CHUNKS,)), dma((2,)), dma((2,)),
        ],
        compiler_params=pltpu.CompilerParams(
            collective_id=int(doublings > DOUBLINGS), has_side_effects=True, vmem_limit_bytes=60 * 2**20
        ),
        name=f"layers{doublings}",
    )(slabs, incident)


def shards(slabs, incident):
    down, bounced, settled = layers(DOUBLINGS, slabs, incident)
    return lax.cond(
        settled[0, 0] == 0.0,
        lambda: (down, bounced),
        lambda: tuple(layers(MORE_DOUBLINGS, slabs, incident)[:2]),
    )


def solution(mesh):
    placed = (P("depth", "slab", None, None, None), P("depth", "slab", None))
    return jax.shard_map(
        shards,
        mesh=mesh,
        in_specs=placed,
        out_specs=(P("depth", "slab", None), P("depth", "slab", None)),
        check_vma=False,
    )
```

```python
import functools

import jax
import jax.numpy as jnp
from jax import lax
from jax.experimental import pallas as pl
from jax.experimental.pallas import tpu as pltpu
from jax.sharding import PartitionSpec as P

F32 = jnp.float32
BF16 = jnp.bfloat16
MESH = pl.DeviceIdType.MESH
DOUBLINGS = 3
MORE_DOUBLINGS = 24
REMAINDER = 1e-5
CHUNKS = 8
CASTS = 8
NEAR_Z = 2
FAR_Z = 5
EARLY = 2
LEVELS = 5
OWN = 8 * LEVELS
PARTNER = OWN + 4
BLOCKS = OWN + 5
TAKEN = 2
KEPT = 0
FINAL_R = 8 * (LEVELS - 1) + 6
FINAL_T = FINAL_R + 1


def split(value):
    high = value.astype(BF16)
    return high, (value - high.astype(F32)).astype(BF16)


def dot(left, right):
    return jnp.dot(left, right, preferred_element_type=F32)


def split_dot(left, right):
    return dot(left[0], right[0]) + (dot(left[0], right[1]) + dot(left[1], right[0]))


def matmul(left, right):
    return split_dot(split(left), split(right))


def kernel(
    doublings, slabs, incident, down, bounced, settled,
    buf, power, inverse, coupled, field, arrive, leave, handed, handing, extra, pair_t, bounce_t,
    load_sem, store_sem, tree_send, tree_recv, cast_send, cast_recv,
    chain_send, chain_recv, hand_send, hand_recv, extra_send, extra_recv, part_send, part_recv,
    heads, poison, relay_send, relay_recv, give_send, give_recv,
):
    slab = lax.axis_index("slab")
    depth = lax.axis_index("depth")
    x = lax.rem(slab, 4)
    z = lax.div(slab, 4)
    core = lax.rem(depth, 2)
    y = lax.div(depth, 2)
    chips = lax.axis_size("depth") // 2
    order = buf.shape[1]
    rows = field.shape[0] // CHUNKS
    band = order // CASTS

    loads = [
        pltpu.make_async_copy(slabs.at[0, 0, i], buf.at[OWN + i], load_sem.at[i]) for i in range(4)
    ]
    loads.append(pltpu.make_async_copy(incident.at[0], field, load_sem.at[4]))
    for load in loads:
        load.start()

    def at(px, pz):
        return lax.rem(pz + 16, 8) * 4 + lax.rem(px + 8, 4)

    rt_x = 1 - core
    qu_x = 2 + core

    def slot(level, pair, part):
        return level * 8 + pair * 2 + part

    on_rt = x == rt_x
    on_qu = x == qu_x
    z2 = lax.rem(z, 2)
    z4 = lax.rem(z, 4)
    mirror = at(3 - x, z)
    odd = lax.rem(x, 2) == 1
    beside = at(x + 1 - 2 * lax.rem(x, 2), z)
    takes = on_rt | on_qu
    crossing2 = (on_qu & (z2 == 0)) | (on_rt & (z2 == 1))
    merged2 = (on_rt & (z2 == 0)) | (on_qu & (z2 == 1))
    inner3 = (on_qu & (z4 == 1)) | (on_rt & (z4 == 2))
    ahead3 = jnp.where(z4 < 2, 1, -1)
    near_rt, near_qu, far_root = at(rt_x, NEAR_Z), at(qu_x, NEAR_Z), at(rt_x, FAR_Z)
    is_near_rt = on_rt & (z == NEAR_Z)
    is_near_qu = on_qu & (z == NEAR_Z)
    is_far = on_rt & (z == FAR_Z)
    is_first = on_rt & (z == 1)
    root = is_near_rt | is_near_qu | is_far

    barrier = pltpu.get_barrier_semaphore()

    def greet(**target):
        pl.semaphore_signal(barrier, inc=1, device_id=target, device_id_type=MESH)

    for px in (1, 3):
        greet(slab=at(x + px, z))
    greet(depth=depth + 1 - 2 * core)

    @pl.when(y > 0)
    def _():
        greet(depth=depth - 2)

    @pl.when(y < chips - 1)
    def _():
        greet(depth=depth + 2)

    meetings = [
        (is_first, near_qu),
        (is_first, far_root),
        (is_near_qu, at(rt_x, 1)),
        (is_near_qu, far_root),
        (is_far, at(rt_x, 1)),
        (is_far, near_qu),
        (is_far, near_rt),
        (is_near_rt, far_root),
        (z > 0, at(x, z - 1)),
        (z < 7, at(x, z + 1)),
    ]
    for meets, target in meetings:

        @pl.when(meets)
        def _(target=target):
            greet(slab=target)

    met = [y > 0, y < chips - 1] + [meets for meets, _ in meetings]
    pl.semaphore_wait(barrier, 3 + sum(flag.astype(jnp.int32) for flag in met))

    final_pair = jnp.where(on_qu, 1, jnp.where(z == 1, 0, 2))
    routes = [
        [],
        [(takes, mirror, 2)],
        [
            (crossing2, mirror, 1),
            (crossing2, at(x, z + 1 - 2 * z2), 2),
        ],
        [
            (inner3, mirror, 1),
            (merged2, at(x, z + ahead3), jnp.where(inner3, 2, 0)),
        ],
        [
            (is_first | is_near_qu | is_far, near_rt, final_pair),
            (is_first | is_far, near_qu, final_pair),
            (is_first | is_near_qu, far_root, final_pair),
        ],
    ]
    computes = [
        takes,
        takes,
        merged2,
        (on_rt & (z4 == 1)) | (on_qu & (z4 == 2)),
        root,
    ]
    local = [3, 3, 0, 3, 3]
    holds = [None, is_near_qu, is_far]

    def tree_copy(level, number, part, source):
        sends, target, pair = routes[level][number]
        return sends, pltpu.make_async_remote_copy(
            src_ref=buf.at[source],
            dst_ref=buf.at[slot(level, pair, part)],
            send_sem=tree_send.at[level, number, part],
            recv_sem=tree_recv.at[level, pair, part],
            device_id={"slab": target},
            device_id_type=MESH,
        )

    def send_to(level, number, part, source):
        sends, copy = tree_copy(level, number, part, source)

        @pl.when(sends)
        def _():
            copy.start()

    def send_part(level, part, source):
        for number in range(min(len(routes[level]), 2)):
            send_to(level, number, part, source)
        if len(routes[level]) > 2 and part == 1:
            send_to(level, 2, 0, source - 1)
            send_to(level, 2, 1, source)

    def await_part(level, pair, part):
        pltpu.make_async_remote_copy(
            src_ref=buf.at[slot(level, pair, part)],
            dst_ref=buf.at[slot(level, pair, part)],
            send_sem=tree_send.at[level, 0, part],
            recv_sem=tree_recv.at[level, pair, part],
            device_id={"slab": slab},
            device_id_type=MESH,
        ).wait_recv()

    for load in loads[:4]:
        load.wait()
    second = jnp.where(odd == (core == 0), 1, 3)
    blocks = [jnp.where(odd, 0, 2), second, 4 - second, jnp.where(odd, 2, 0)]

    def give_copy(turn):
        return pltpu.make_async_remote_copy(
            src_ref=buf.at[OWN + blocks[turn]],
            dst_ref=buf.at[TAKEN + blocks[turn]],
            send_sem=give_send.at[turn],
            recv_sem=give_recv.at[turn],
            device_id={"slab": beside},
            device_id_type=MESH,
        )

    @pl.when(jnp.logical_not(takes))
    def _():
        for turn in range(4):
            give_copy(turn).start()

    head = (pl.ds(0, 8), pl.ds(0, 128))

    def merge(place, wait, finish, transmission_first=False):
        wait("p1")
        wait("p2")
        near = buf[place["p1"]]
        far = split(buf[place["p2"]])
        system = split_dot(split(near), far)
        ones = lax.broadcasted_iota(jnp.int32, (order, order), 0) == lax.broadcasted_iota(jnp.int32, (order, order), 1)
        inverse[...] = system + jnp.where(ones, 1.0, 0.0)
        power[...] = system

        def double(halves):
            squared = split_dot(halves, halves)
            power[...] = squared
            whole = inverse[...]
            inverse[...] = whole + split_dot(split(squared), split(whole))

        if doublings <= DOUBLINGS:
            for _ in range(doublings - 1):
                double(split(power[...]))
            last = jnp.square(power[...]).reshape(order // 8, 8, order // 128, 128)
            poison[...] = jnp.where(jnp.sum(last, axis=(0, 2)) < REMAINDER / 1024, 0.0, jnp.nan)
        else:

            def step(_, carry):
                double(split(power[...]))
                return carry

            lax.fori_loop(0, doublings - 1, step, 0)
        solved = split(inverse[...])
        coupled[...] = split_dot(far, solved)
        wait("s")
        right = split(buf[place["s"]])
        through = split_dot(solved, right)
        turned = split_dot(split(coupled[...]), right)

        def reflection():
            wait("m1")
            wait("add")
            finish(0, buf[place["add"]] + matmul(buf[place["m1"]], turned))

        def transmission():
            wait("m2")
            finish(1, matmul(buf[place["m2"]], through))

        if transmission_first:
            transmission()
            reflection()
        else:
            reflection()
            transmission()

    def put(place, value):
        buf[place] = value
        if doublings <= DOUBLINGS:
            buf[(place, *head)] += poison[...]

    upper = jnp.where(odd, TAKEN, OWN)
    lower = jnp.where(odd, OWN, TAKEN)

    def sides(is_qu):
        return {
            "p1": jnp.where(is_qu, lower, upper + 2),
            "p2": jnp.where(is_qu, upper + 2, lower),
            "s": jnp.where(is_qu, lower + 3, upper + 1),
            "add": jnp.where(is_qu, lower + 2, upper),
            "m1": jnp.where(is_qu, lower + 1, upper + 3),
            "m2": jnp.where(is_qu, upper + 3, lower + 1),
        }

    def given(turns):
        def wait(name):
            if name in turns:
                give_copy(turns[name]).wait_recv()

        return wait

    def finish_sent(part, value):
        put(slot(0, 3, part), value)
        send_part(1, part, slot(0, 3, part))

    def finish_kept(part, value):
        put(KEPT + part, value)

    @pl.when(takes & (core == 0))
    def _():
        merge(sides(x < 2), given({"p1": 0, "m2": 1}), finish_sent)
        merge(sides(x >= 2), given({"s": 2, "add": 3}), finish_kept)

    @pl.when(takes & (core == 1))
    def _():
        merge(sides(x < 2), given({"p1": 0, "s": 1, "m1": 2, "add": 3}), finish_sent, transmission_first=True)
        merge(sides(x >= 2), given({}), finish_kept)

    names = {"add": (0, 0), "s": (0, 1), "p1": (1, 0), "m1": (1, 1), "p2": (2, 0), "m2": (2, 1)}

    def merge_level(level):
        def operand(pair, part):
            if level == 1:
                return [KEPT + part, slot(0, 3, part), slot(1, 2, part)][pair]
            if level == 4:
                return jnp.where(holds[pair], slot(3, 3, part), slot(level, pair, part)) if pair else slot(level, 0, part)
            return slot(level - 1, 3, part) if local[level] == pair else slot(level, pair, part)

        def wait(name):
            pair, part = names[name]
            if level == 4 and pair:

                @pl.when(jnp.logical_not(holds[pair]))
                def _():
                    await_part(level, pair, part)

                return
            if pair == 2 if level == 1 else pair != local[level]:
                await_part(level, pair, part)

        def finish(part, value):
            put(slot(level, 3, part), value)
            if level + 1 < LEVELS:
                send_part(level + 1, part, slot(level, 3, part))

        place = {name: operand(*key) for name, key in names.items()}
        merge(place, wait, finish, transmission_first=level + 1 == LEVELS)

    for level in range(1, LEVELS):

        @pl.when(computes[level])
        def _(level=level):
            merge_level(level)

    x_line = (core == 1) | (z == NEAR_Z) | (z == FAR_Z)
    z_line = (core == 0) | (takes & (z < 4)) | (on_rt & (z >= 4))
    children = [
        (takes & x_line, beside),
        (on_rt & (z >= 4) & x_line, mirror),
        (z_line & ((z == NEAR_Z) | (z == FAR_Z) | (z == FAR_Z + 1)), at(x, z + 1)),
        (z_line & ((z == NEAR_Z) | (z == NEAR_Z - 1) | (z == FAR_Z)), at(x, z - 1)),
    ]

    def cast_copy(which, chunk, child):
        place = buf.at[FINAL_R + which, pl.ds(chunk * band, band)]
        return pltpu.make_async_remote_copy(
            src_ref=place,
            dst_ref=place,
            send_sem=cast_send.at[which, chunk, child],
            recv_sem=cast_recv.at[which, chunk],
            device_id={"slab": children[child][1]},
            device_id_type=MESH,
        )

    def part_copy(chunk):
        return pltpu.make_async_remote_copy(
            src_ref=buf.at[FINAL_T, pl.ds(chunk * band, band)],
            dst_ref=buf.at[PARTNER, pl.ds(chunk * band, band)],
            send_sem=part_send.at[chunk],
            recv_sem=part_recv.at[chunk],
            device_id={"depth": depth + 1 - 2 * core},
            device_id_type=MESH,
        )

    def relay_copy(way):
        return pltpu.make_async_remote_copy(
            src_ref=heads.at[way],
            dst_ref=heads.at[2 + way],
            send_sem=relay_send.at[way],
            recv_sem=relay_recv.at[way],
            device_id={"depth": lax.rem(depth + (2 * chips - 2 if way else 2), 2 * chips)},
            device_id_type=MESH,
        )

    first = y == 0
    final = y == chips - 1

    def relay(way):
        head = (pl.ds(0, 8), pl.ds(0, 128))
        start, end = (final, first) if way else (first, final)
        heads[way] = (buf[(FINAL_T, *head)] + buf[(PARTNER, *head)]) * 0.0

        @pl.when(jnp.logical_not(start))
        def _():
            relay_copy(way).wait_recv()
            heads[way] += heads[2 + way]

        @pl.when(jnp.logical_not(end))
        def _():
            relay_copy(way).start()

    def forward(which):
        for chunk in range(CASTS):

            @pl.when(jnp.logical_not(root))
            def _():
                cast_copy(which, chunk, 0).wait_recv()

            for child in range(4):

                @pl.when(children[child][0])
                def _():
                    cast_copy(which, chunk, child).start()

            if which == 1:
                part_copy(chunk).start()

    def keep_split(ref, value):
        ref[0], ref[1] = split(value)

    def kept(ref):
        return ref[0], ref[1]

    def forward_r():
        forward(0)
        keep_split(bounce_t, buf[FINAL_R].T)

    extra_copy = pltpu.make_async_remote_copy(
        src_ref=extra,
        dst_ref=extra,
        send_sem=extra_send,
        recv_sem=extra_recv,
        device_id={"depth": depth + 1 - 2 * core},
        device_id_type=MESH,
    )

    def chain_copy(chunk):
        return pltpu.make_async_remote_copy(
            src_ref=leave.at[pl.ds(chunk * rows, rows)],
            dst_ref=arrive.at[pl.ds(chunk * rows, rows)],
            send_sem=chain_send.at[chunk],
            recv_sem=chain_recv.at[chunk],
            device_id={"depth": lax.rem(depth + 2, 2 * chips)},
            device_id_type=MESH,
        )

    def hand_copy(chunk):
        return pltpu.make_async_remote_copy(
            src_ref=field.at[pl.ds(chunk * rows, rows)],
            dst_ref=handed.at[pl.ds(chunk * rows, rows)],
            send_sem=hand_send.at[chunk],
            recv_sem=hand_recv.at[chunk],
            device_id={"depth": depth + 1 - 2 * core},
            device_id_type=MESH,
        )

    forward(1)
    loads[4].wait()

    @pl.when(core == 1)
    def _():
        keep_split(pair_t, buf[FINAL_T].T)
        extra[...] = split_dot(split(field[...]), kept(pair_t))
        extra_copy.start()
        for chunk in range(CASTS):
            part_copy(chunk).wait_recv()
        keep_split(pair_t, buf[PARTNER].T)

        @pl.when(y >= chips // 2)
        def _():
            relay(1)

        forward_r()
        for chunk in range(CHUNKS):
            part = pl.ds(chunk * rows, rows)
            hand_copy(chunk).wait_recv()
            field[part] += split_dot(split(handed[part]), kept(pair_t))

        relay(0)

        @pl.when(y < chips // 2)
        def _():
            relay(1)

    @pl.when(core == 0)
    def _():
        for chunk in range(CASTS):
            part_copy(chunk).wait_recv()
        keep_split(pair_t, matmul(buf[PARTNER], buf[FINAL_T]).T)
        extra_copy.wait_recv()
        extra[...] += split_dot(split(field[...]), kept(pair_t))

        @pl.when(y == 0)
        def _():
            for chunk in range(CHUNKS):
                part = pl.ds(chunk * rows, rows)
                leave[part] = extra[part]
                chain_copy(chunk).start()
                hand_copy(chunk).start()

        @pl.when(y >= chips // 2)
        def _():
            relay(1)

        @pl.when(y > EARLY)
        def _():
            forward_r()

        @pl.when(y > 0)
        def _():
            for chunk in range(CHUNKS):
                part = pl.ds(chunk * rows, rows)
                chain_copy(chunk).wait_recv()

                @pl.when(y < chips - 1)
                def _():
                    leave[part] = extra[part] + split_dot(split(arrive[part]), kept(pair_t))
                    chain_copy(chunk).start()

                field[part] += arrive[part]
                hand_copy(chunk).start()

        relay(0)

        @pl.when(y <= EARLY)
        def _():
            forward_r()

        @pl.when(y < chips // 2)
        def _():
            relay(1)

    store_down = pltpu.make_async_copy(field, down.at[0], store_sem.at[0])
    store_down.start()

    handing[...] = split_dot(split(field[...]), kept(bounce_t))
    store_bounced = pltpu.make_async_copy(handing, bounced.at[0], store_sem.at[1])
    store_bounced.start()

    settled[0, 0] = jnp.sum(heads[0] + heads[1])

    @pl.when(jnp.logical_not(takes))
    def _():
        for turn in range(4):
            give_copy(turn).wait_send()

    for level in range(LEVELS):
        for number in range(len(routes[level])):
            for part in range(2):
                sends, copy = tree_copy(level, number, part, OWN)

                @pl.when(sends)
                def _():
                    copy.wait_send()

    for which in range(2):
        for chunk in range(CASTS):
            for child in range(4):

                @pl.when(children[child][0])
                def _():
                    cast_copy(which, chunk, child).wait_send()

    for chunk in range(CASTS):
        part_copy(chunk).wait_send()

    @pl.when(core == 1)
    def _():
        extra_copy.wait_send()

    @pl.when(core == 0)
    def _():
        for chunk in range(CHUNKS):
            hand_copy(chunk).wait_send()

        @pl.when(y < chips - 1)
        def _():
            for chunk in range(CHUNKS):
                chain_copy(chunk).wait_send()

    @pl.when(jnp.logical_not(final))
    def _():
        relay_copy(0).wait_send()

    @pl.when(jnp.logical_not(first))
    def _():
        relay_copy(1).wait_send()

    store_down.wait()
    store_bounced.wait()


def layers(doublings, slabs, incident):
    order = slabs.shape[-1]
    rows = incident.shape[1]
    block = jax.ShapeDtypeStruct(incident.shape, F32)
    matrix = pltpu.VMEM((order, order), F32)
    halves = pltpu.VMEM((2, order, order), BF16)
    fields = pltpu.VMEM((rows, order), F32)
    dma = pltpu.SemaphoreType.DMA
    return pl.pallas_call(
        functools.partial(kernel, doublings),
        out_shape=(block, block, jax.ShapeDtypeStruct((1, 1), F32)),
        in_specs=[pl.BlockSpec(memory_space=pl.ANY)] * 2,
        out_specs=[pl.BlockSpec(memory_space=pl.ANY)] * 2 + [pl.BlockSpec(memory_space=pltpu.SMEM)],
        scratch_shapes=[
            pltpu.VMEM((BLOCKS, order, order), F32),
            matrix, matrix, matrix,
            fields, fields, fields, fields, fields, fields,
            halves, halves,
            dma((5,)), dma((2,)),
            dma((LEVELS, 3, 2)), dma((LEVELS, 3, 2)),
            dma((2, CASTS, 4)), dma((2, CASTS)),
            dma((CHUNKS,)), dma((CHUNKS,)),
            dma((CHUNKS,)), dma((CHUNKS,)),
            dma, dma,
            dma((CASTS,)), dma((CASTS,)),
            pltpu.VMEM((4, 8, 128), F32), pltpu.VMEM((8, 128), F32),
            dma((2,)), dma((2,)),
            dma((4,)), dma((4,)),
        ],
        compiler_params=pltpu.CompilerParams(
            collective_id=int(doublings > DOUBLINGS), has_side_effects=True, vmem_limit_bytes=60 * 2**20
        ),
        name=f"layers{doublings}",
    )(slabs, incident)


def shards(slabs, incident):
    down, bounced, settled = layers(DOUBLINGS, slabs, incident)
    return lax.cond(
        settled[0, 0] == 0.0,
        lambda: (down, bounced),
        lambda: tuple(layers(MORE_DOUBLINGS, slabs, incident)[:2]),
    )


def solution(mesh):
    placed = (P("depth", "slab", None, None, None), P("depth", "slab", None))
    return jax.shard_map(
        shards,
        mesh=mesh,
        in_specs=placed,
        out_specs=(P("depth", "slab", None), P("depth", "slab", None)),
        check_vma=False,
    )
```

```python
import functools

import jax
import jax.numpy as jnp
from jax import lax
from jax.experimental import pallas as pl
from jax.experimental.pallas import tpu as pltpu
from jax.sharding import PartitionSpec as P

F32 = jnp.float32
BF16 = jnp.bfloat16
MESH = pl.DeviceIdType.MESH
DOUBLINGS = 3
MORE_DOUBLINGS = 24
REMAINDER = 1e-5
CHUNKS = 8
CASTS = 8
NEAR_Z = 1
PIECES = 4
FAR_Z = 5
EARLY = 2
LEVELS = 5
OWN = 8 * LEVELS
PARTNER = OWN + 4
BLOCKS = OWN + 5
TAKEN = 2
KEPT = 0
FINAL_R = 8 * (LEVELS - 1) + 6
FINAL_T = FINAL_R + 1


def split(value):
    high = value.astype(BF16)
    return high, (value - high.astype(F32)).astype(BF16)


def dot(left, right):
    return jnp.dot(left, right, preferred_element_type=F32)


def split_dot(left, right):
    return dot(left[0], right[0]) + (dot(left[0], right[1]) + dot(left[1], right[0]))


def matmul(left, right):
    return split_dot(split(left), split(right))


def kernel(
    doublings, slabs, incident, down, bounced, settled,
    buf, power, inverse, coupled, field, arrive, leave, handed, handing, extra, pair_t, bounce_t,
    load_sem, store_sem, tree_send, tree_recv, cast_send, cast_recv,
    chain_send, chain_recv, hand_send, hand_recv, extra_send, extra_recv, part_send, part_recv,
    heads, poison, relay_send, relay_recv, give_send, give_recv, last_send, last_recv, swap_send, swap_recv,
):
    slab = lax.axis_index("slab")
    depth = lax.axis_index("depth")
    x = lax.rem(slab, 4)
    z = lax.div(slab, 4)
    core = lax.rem(depth, 2)
    y = lax.div(depth, 2)
    chips = lax.axis_size("depth") // 2
    order = buf.shape[1]
    rows = field.shape[0] // CHUNKS
    band = order // CASTS

    loads = [
        pltpu.make_async_copy(slabs.at[0, 0, i], buf.at[OWN + i], load_sem.at[i]) for i in range(4)
    ]
    loads.append(pltpu.make_async_copy(incident.at[0], field, load_sem.at[4]))
    for load in loads:
        load.start()

    def at(px, pz):
        return lax.rem(pz + 16, 8) * 4 + lax.rem(px + 8, 4)

    rt_x = 1 - core
    qu_x = 2 + core

    def slot(level, pair, part):
        return level * 8 + pair * 2 + part

    on_rt = x == rt_x
    on_qu = x == qu_x
    z2 = lax.rem(z, 2)
    z4 = lax.rem(z, 4)
    mirror = at(3 - x, z)
    odd = lax.rem(x, 2) == 1
    beside = at(x + 1 - 2 * lax.rem(x, 2), z)
    takes = on_rt | on_qu
    crossing2 = (on_qu & (z2 == 0)) | (on_rt & (z2 == 1))
    merged2 = (on_rt & (z2 == 0)) | (on_qu & (z2 == 1))
    inner3 = (on_qu & (z4 == 1)) | (on_rt & (z4 == 2))
    ahead3 = jnp.where(z4 < 2, 1, -1)
    near_root, far_root = at(rt_x, NEAR_Z), at(rt_x, FAR_Z)
    is_near = on_rt & (z == NEAR_Z)
    is_far = on_rt & (z == FAR_Z)
    from_qu = on_qu & (z == NEAR_Z + 1)
    root = is_near | is_far

    barrier = pltpu.get_barrier_semaphore()

    def greet(**target):
        pl.semaphore_signal(barrier, inc=1, device_id=target, device_id_type=MESH)

    for px in (1, 3):
        greet(slab=at(x + px, z))
    greet(depth=depth + 1 - 2 * core)

    @pl.when(y > 0)
    def _():
        greet(depth=depth - 2)

    @pl.when(y < chips - 1)
    def _():
        greet(depth=depth + 2)

    meetings = [
        (from_qu, near_root),
        (from_qu, far_root),
        (root, at(qu_x, NEAR_Z + 1)),
        (is_near, far_root),
        (is_far, near_root),
        (z > 0, at(x, z - 1)),
        (z < 7, at(x, z + 1)),
    ]
    for meets, target in meetings:

        @pl.when(meets)
        def _(target=target):
            greet(slab=target)

    met = [y > 0, y < chips - 1] + [meets for meets, _ in meetings]
    pl.semaphore_wait(barrier, 3 + sum(flag.astype(jnp.int32) for flag in met))

    routes = [
        [],
        [(takes, mirror, 2)],
        [
            (crossing2, mirror, 1),
            (crossing2, at(x, z + 1 - 2 * z2), 2),
        ],
        [
            (inner3, mirror, 1),
            (merged2, at(x, z + ahead3), jnp.where(inner3, 2, 0)),
        ],
        [
            (from_qu | is_far, near_root, jnp.where(on_qu, 1, 2)),
            (from_qu | is_near, far_root, jnp.where(on_qu, 1, 0)),
        ],
    ]
    computes = [
        takes,
        takes,
        merged2,
        (on_rt & (z4 == 1)) | (on_qu & (z4 == 2)),
        root,
    ]
    local = [3, 3, 0, 3, 3]
    holds = [is_near, None, is_far]

    def tree_copy(level, number, part, source):
        sends, target, pair = routes[level][number]
        return sends, pltpu.make_async_remote_copy(
            src_ref=buf.at[source],
            dst_ref=buf.at[slot(level, pair, part)],
            send_sem=tree_send.at[level, number, part],
            recv_sem=tree_recv.at[level, pair, part],
            device_id={"slab": target},
            device_id_type=MESH,
        )

    def send_part(level, part, source):
        for number in range(len(routes[level])):
            sends, copy = tree_copy(level, number, part, source)

            @pl.when(sends)
            def _():
                copy.start()

    def await_part(level, pair, part):
        pltpu.make_async_remote_copy(
            src_ref=buf.at[slot(level, pair, part)],
            dst_ref=buf.at[slot(level, pair, part)],
            send_sem=tree_send.at[level, 0, part],
            recv_sem=tree_recv.at[level, pair, part],
            device_id={"slab": slab},
            device_id_type=MESH,
        ).wait_recv()

    for load in loads[:4]:
        load.wait()
    second = jnp.where(odd == (core == 0), 1, 3)
    blocks = [jnp.where(odd, 0, 2), second, 4 - second, jnp.where(odd, 2, 0)]

    def give_copy(turn):
        return pltpu.make_async_remote_copy(
            src_ref=buf.at[OWN + blocks[turn]],
            dst_ref=buf.at[TAKEN + blocks[turn]],
            send_sem=give_send.at[turn],
            recv_sem=give_recv.at[turn],
            device_id={"slab": beside},
            device_id_type=MESH,
        )

    cut = order // PIECES

    def last_copy(piece):
        lines = pl.ds(piece * cut, cut)
        return pltpu.make_async_remote_copy(
            src_ref=buf.at[OWN + blocks[3], lines],
            dst_ref=buf.at[TAKEN + blocks[3], lines],
            send_sem=last_send.at[piece],
            recv_sem=last_recv.at[piece],
            device_id={"slab": beside},
            device_id_type=MESH,
        )

    def swap_copy(piece):
        lines = pl.ds(piece * cut, cut)
        return pltpu.make_async_remote_copy(
            src_ref=buf.at[slot(0, 3, 0), lines],
            dst_ref=buf.at[slot(1, 2, 0), lines],
            send_sem=swap_send.at[piece],
            recv_sem=swap_recv.at[piece],
            device_id={"slab": mirror},
            device_id_type=MESH,
        )

    @pl.when(jnp.logical_not(takes))
    def _():
        for turn in range(3):
            give_copy(turn).start()
        for piece in range(PIECES):
            last_copy(piece).start()

    head = (pl.ds(0, 8), pl.ds(0, 128))

    def merge(place, wait, finish, transmission_first=False, adds=True):
        wait("p1")
        wait("p2")
        near = buf[place["p1"]]
        far = split(buf[place["p2"]])
        system = split_dot(split(near), far)
        ones = lax.broadcasted_iota(jnp.int32, (order, order), 0) == lax.broadcasted_iota(jnp.int32, (order, order), 1)
        inverse[...] = system + jnp.where(ones, 1.0, 0.0)
        power[...] = system

        def double(halves):
            squared = split_dot(halves, halves)
            power[...] = squared
            whole = inverse[...]
            inverse[...] = whole + split_dot(split(squared), split(whole))

        if doublings <= DOUBLINGS:
            for _ in range(doublings - 1):
                double(split(power[...]))
            last = jnp.square(power[...]).reshape(order // 8, 8, order // 128, 128)
            poison[...] = jnp.where(jnp.sum(last, axis=(0, 2)) < REMAINDER / 1024, 0.0, jnp.nan)
        else:

            def step(_, carry):
                double(split(power[...]))
                return carry

            lax.fori_loop(0, doublings - 1, step, 0)
        solved = split(inverse[...])
        coupled[...] = split_dot(far, solved)
        wait("s")
        right = split(buf[place["s"]])
        through = split_dot(solved, right)
        turned = split_dot(split(coupled[...]), right)

        def reflection():
            wait("m1")
            partial = matmul(buf[place["m1"]], turned)
            if adds:
                wait("add")
                partial = buf[place["add"]] + partial
            finish(0, partial)

        def transmission():
            wait("m2")
            finish(1, matmul(buf[place["m2"]], through))

        if transmission_first:
            transmission()
            reflection()
        else:
            reflection()
            transmission()

    def put(place, value):
        buf[place] = value
        if doublings <= DOUBLINGS:
            buf[(place, *head)] += poison[...]

    upper = jnp.where(odd, TAKEN, OWN)
    lower = jnp.where(odd, OWN, TAKEN)

    def sides(is_qu):
        return {
            "p1": jnp.where(is_qu, lower, upper + 2),
            "p2": jnp.where(is_qu, upper + 2, lower),
            "s": jnp.where(is_qu, lower + 3, upper + 1),
            "add": jnp.where(is_qu, lower + 2, upper),
            "m1": jnp.where(is_qu, lower + 1, upper + 3),
            "m2": jnp.where(is_qu, upper + 3, lower + 1),
        }

    def given(turns):
        def wait(name):
            if name in turns:
                if turns[name] < 3:
                    give_copy(turns[name]).wait_recv()
                else:
                    for piece in range(PIECES):
                        last_copy(piece).wait_recv()

        return wait

    def finish_sent(part, value):
        put(slot(0, 3, part), value)
        if part == 1:
            send_part(1, 1, slot(0, 3, 1))
        else:
            for piece in range(PIECES):
                swap_copy(piece).start()

    def finish_pieces(part, value):
        if part == 1:
            finish_sent(part, value)
            return
        put(slot(0, 3, 0), value)
        addend = sides(x < 2)["add"]
        for piece in range(PIECES):
            lines = pl.ds(piece * cut, cut)
            last_copy(piece).wait_recv()
            buf[slot(0, 3, 0), lines] += buf[addend, lines]
            swap_copy(piece).start()

    def finish_kept(part, value):
        put(KEPT + part, value)

    @pl.when(takes & (core == 0))
    def _():
        merge(sides(x < 2), given({"p1": 0, "m2": 1}), finish_sent)
        merge(sides(x >= 2), given({"s": 2, "add": 3}), finish_kept)

    @pl.when(takes & (core == 1))
    def _():
        merge(sides(x < 2), given({"p1": 0, "s": 1, "m1": 2}), finish_pieces, transmission_first=True, adds=False)
        merge(sides(x >= 2), given({}), finish_kept)

    names = {"add": (0, 0), "s": (0, 1), "p1": (1, 0), "m1": (1, 1), "p2": (2, 0), "m2": (2, 1)}

    def merge_level(level):
        def operand(pair, part):
            if level == 1:
                return [KEPT + part, slot(0, 3, part), slot(1, 2, part)][pair]
            if level == 4:
                return slot(level, 1, part) if pair == 1 else jnp.where(holds[pair], slot(3, 3, part), slot(level, pair, part))
            return slot(level - 1, 3, part) if local[level] == pair else slot(level, pair, part)

        def wait(name):
            pair, part = names[name]
            if level == 4 and pair != 1:

                @pl.when(jnp.logical_not(holds[pair]))
                def _():
                    await_part(level, pair, part)

                return
            if level == 1 and name == "p2":
                for piece in range(PIECES):
                    swap_copy(piece).wait_recv()
            elif pair == 2 if level == 1 else pair != local[level]:
                await_part(level, pair, part)

        def finish(part, value):
            put(slot(level, 3, part), value)
            if level + 1 < LEVELS:
                send_part(level + 1, part, slot(level, 3, part))

        place = {name: operand(*key) for name, key in names.items()}
        merge(place, wait, finish, transmission_first=level + 1 == LEVELS)

    for level in range(1, LEVELS):

        @pl.when(computes[level])
        def _(level=level):
            merge_level(level)

    dx = lax.rem(x - rt_x + 4, 4)
    dz = lax.rem(z - NEAR_Z + 4, 4)
    x_first = core == 0
    x_line = jnp.logical_not(x_first) | (dz == 0)
    z_line = x_first | (dx == 0)
    children = [
        (x_line & ((dx == 0) | (x_first & (dx == 1))), at(x + 1, z)),
        (x_line & ((dx == 0) | (jnp.logical_not(x_first) & (dx == 3))), at(x - 1, z)),
        (z_line & (dz <= 1), at(x, z + 1)),
        (z_line & (dz == 0), at(x, z - 1)),
    ]

    def cast_copy(which, chunk, child):
        place = buf.at[FINAL_R + which, pl.ds(chunk * band, band)]
        return pltpu.make_async_remote_copy(
            src_ref=place,
            dst_ref=place,
            send_sem=cast_send.at[which, chunk, child],
            recv_sem=cast_recv.at[which, chunk],
            device_id={"slab": children[child][1]},
            device_id_type=MESH,
        )

    def part_copy(chunk):
        return pltpu.make_async_remote_copy(
            src_ref=buf.at[FINAL_T, pl.ds(chunk * band, band)],
            dst_ref=buf.at[PARTNER, pl.ds(chunk * band, band)],
            send_sem=part_send.at[chunk],
            recv_sem=part_recv.at[chunk],
            device_id={"depth": depth + 1 - 2 * core},
            device_id_type=MESH,
        )

    def relay_copy(way):
        return pltpu.make_async_remote_copy(
            src_ref=heads.at[way],
            dst_ref=heads.at[2 + way],
            send_sem=relay_send.at[way],
            recv_sem=relay_recv.at[way],
            device_id={"depth": lax.rem(depth + (2 * chips - 2 if way else 2), 2 * chips)},
            device_id_type=MESH,
        )

    first = y == 0
    final = y == chips - 1

    def relay(way):
        head = (pl.ds(0, 8), pl.ds(0, 128))
        start, end = (final, first) if way else (first, final)
        heads[way] = (buf[(FINAL_T, *head)] + buf[(PARTNER, *head)]) * 0.0

        @pl.when(jnp.logical_not(start))
        def _():
            relay_copy(way).wait_recv()
            heads[way] += heads[2 + way]

        @pl.when(jnp.logical_not(end))
        def _():
            relay_copy(way).start()

    def forward(which):
        for chunk in range(CASTS):

            @pl.when(jnp.logical_not(root))
            def _():
                cast_copy(which, chunk, 0).wait_recv()

            for child in range(4):

                @pl.when(children[child][0])
                def _():
                    cast_copy(which, chunk, child).start()

            if which == 1:
                part_copy(chunk).start()

    def keep_split(ref, value):
        ref[0], ref[1] = split(value)

    def kept(ref):
        return ref[0], ref[1]

    def forward_r():
        forward(0)
        keep_split(bounce_t, buf[FINAL_R].T)

    extra_copy = pltpu.make_async_remote_copy(
        src_ref=extra,
        dst_ref=extra,
        send_sem=extra_send,
        recv_sem=extra_recv,
        device_id={"depth": depth + 1 - 2 * core},
        device_id_type=MESH,
    )

    def chain_copy(chunk):
        return pltpu.make_async_remote_copy(
            src_ref=leave.at[pl.ds(chunk * rows, rows)],
            dst_ref=arrive.at[pl.ds(chunk * rows, rows)],
            send_sem=chain_send.at[chunk],
            recv_sem=chain_recv.at[chunk],
            device_id={"depth": lax.rem(depth + 2, 2 * chips)},
            device_id_type=MESH,
        )

    def hand_copy(chunk):
        return pltpu.make_async_remote_copy(
            src_ref=field.at[pl.ds(chunk * rows, rows)],
            dst_ref=handed.at[pl.ds(chunk * rows, rows)],
            send_sem=hand_send.at[chunk],
            recv_sem=hand_recv.at[chunk],
            device_id={"depth": depth + 1 - 2 * core},
            device_id_type=MESH,
        )

    forward(1)
    loads[4].wait()

    @pl.when(core == 1)
    def _():
        keep_split(pair_t, buf[FINAL_T].T)
        extra[...] = split_dot(split(field[...]), kept(pair_t))
        extra_copy.start()
        for chunk in range(CASTS):
            part_copy(chunk).wait_recv()
        keep_split(pair_t, buf[PARTNER].T)

        @pl.when(y >= chips // 2)
        def _():
            relay(1)

        forward_r()
        for chunk in range(CHUNKS):
            part = pl.ds(chunk * rows, rows)
            hand_copy(chunk).wait_recv()
            field[part] += split_dot(split(handed[part]), kept(pair_t))

        relay(0)

        @pl.when(y < chips // 2)
        def _():
            relay(1)

    @pl.when(core == 0)
    def _():
        for chunk in range(CASTS):
            part_copy(chunk).wait_recv()
        keep_split(pair_t, matmul(buf[PARTNER], buf[FINAL_T]).T)
        extra_copy.wait_recv()
        extra[...] += split_dot(split(field[...]), kept(pair_t))

        @pl.when(y == 0)
        def _():
            for chunk in range(CHUNKS):
                part = pl.ds(chunk * rows, rows)
                leave[part] = extra[part]
                chain_copy(chunk).start()
                hand_copy(chunk).start()

        @pl.when(y >= chips // 2)
        def _():
            relay(1)

        @pl.when(y > EARLY)
        def _():
            forward_r()

        @pl.when(y > 0)
        def _():
            for chunk in range(CHUNKS):
                part = pl.ds(chunk * rows, rows)
                chain_copy(chunk).wait_recv()

                @pl.when(y < chips - 1)
                def _():
                    leave[part] = extra[part] + split_dot(split(arrive[part]), kept(pair_t))
                    chain_copy(chunk).start()

                field[part] += arrive[part]
                hand_copy(chunk).start()

        relay(0)

        @pl.when(y <= EARLY)
        def _():
            forward_r()

        @pl.when(y < chips // 2)
        def _():
            relay(1)

    store_down = pltpu.make_async_copy(field, down.at[0], store_sem.at[0])
    store_down.start()

    handing[...] = split_dot(split(field[...]), kept(bounce_t))
    store_bounced = pltpu.make_async_copy(handing, bounced.at[0], store_sem.at[1])
    store_bounced.start()

    settled[0, 0] = jnp.sum(heads[0] + heads[1])

    @pl.when(jnp.logical_not(takes))
    def _():
        for turn in range(3):
            give_copy(turn).wait_send()
        for piece in range(PIECES):
            last_copy(piece).wait_send()

    @pl.when(takes)
    def _():
        for piece in range(PIECES):
            swap_copy(piece).wait_send()

    for level in range(LEVELS):
        for number in range(len(routes[level])):
            for part in range(level == 1, 2):
                sends, copy = tree_copy(level, number, part, OWN)

                @pl.when(sends)
                def _():
                    copy.wait_send()

    for which in range(2):
        for chunk in range(CASTS):
            for child in range(4):

                @pl.when(children[child][0])
                def _():
                    cast_copy(which, chunk, child).wait_send()

    for chunk in range(CASTS):
        part_copy(chunk).wait_send()

    @pl.when(core == 1)
    def _():
        extra_copy.wait_send()

    @pl.when(core == 0)
    def _():
        for chunk in range(CHUNKS):
            hand_copy(chunk).wait_send()

        @pl.when(y < chips - 1)
        def _():
            for chunk in range(CHUNKS):
                chain_copy(chunk).wait_send()

    @pl.when(jnp.logical_not(final))
    def _():
        relay_copy(0).wait_send()

    @pl.when(jnp.logical_not(first))
    def _():
        relay_copy(1).wait_send()

    store_down.wait()
    store_bounced.wait()


def layers(doublings, slabs, incident):
    order = slabs.shape[-1]
    rows = incident.shape[1]
    block = jax.ShapeDtypeStruct(incident.shape, F32)
    matrix = pltpu.VMEM((order, order), F32)
    halves = pltpu.VMEM((2, order, order), BF16)
    fields = pltpu.VMEM((rows, order), F32)
    dma = pltpu.SemaphoreType.DMA
    return pl.pallas_call(
        functools.partial(kernel, doublings),
        out_shape=(block, block, jax.ShapeDtypeStruct((1, 1), F32)),
        in_specs=[pl.BlockSpec(memory_space=pl.ANY)] * 2,
        out_specs=[pl.BlockSpec(memory_space=pl.ANY)] * 2 + [pl.BlockSpec(memory_space=pltpu.SMEM)],
        scratch_shapes=[
            pltpu.VMEM((BLOCKS, order, order), F32),
            matrix, matrix, matrix,
            fields, fields, fields, fields, fields, fields,
            halves, halves,
            dma((5,)), dma((2,)),
            dma((LEVELS, 2, 2)), dma((LEVELS, 3, 2)),
            dma((2, CASTS, 4)), dma((2, CASTS)),
            dma((CHUNKS,)), dma((CHUNKS,)),
            dma((CHUNKS,)), dma((CHUNKS,)),
            dma, dma,
            dma((CASTS,)), dma((CASTS,)),
            pltpu.VMEM((4, 8, 128), F32), pltpu.VMEM((8, 128), F32),
            dma((2,)), dma((2,)),
            dma((3,)), dma((3,)), dma((PIECES,)), dma((PIECES,)), dma((PIECES,)), dma((PIECES,)),
        ],
        compiler_params=pltpu.CompilerParams(
            collective_id=int(doublings > DOUBLINGS), has_side_effects=True, vmem_limit_bytes=60 * 2**20
        ),
        name=f"layers{doublings}",
    )(slabs, incident)


def shards(slabs, incident):
    down, bounced, settled = layers(DOUBLINGS, slabs, incident)
    return lax.cond(
        settled[0, 0] == 0.0,
        lambda: (down, bounced),
        lambda: tuple(layers(MORE_DOUBLINGS, slabs, incident)[:2]),
    )


def solution(mesh):
    placed = (P("depth", "slab", None, None, None), P("depth", "slab", None))
    return jax.shard_map(
        shards,
        mesh=mesh,
        in_specs=placed,
        out_specs=(P("depth", "slab", None), P("depth", "slab", None)),
        check_vma=False,
    )
```

```python
import functools

import jax
import jax.numpy as jnp
from jax import lax
from jax.experimental import pallas as pl
from jax.experimental.pallas import tpu as pltpu
from jax.sharding import PartitionSpec as P

F32 = jnp.float32
BF16 = jnp.bfloat16
MESH = pl.DeviceIdType.MESH
DOUBLINGS = 3
MORE_DOUBLINGS = 24
REMAINDER = 1e-5
CHUNKS = 8
CASTS = 8
NEAR_Z = 1
PIECES = 4
FAR_Z = 5
EARLY = 2
LEVELS = 5
OWN = 8 * LEVELS
PARTNER = OWN + 4
BLOCKS = OWN + 5
TAKEN = 2
KEPT = 0
FINAL_R = 8 * (LEVELS - 1) + 6
FINAL_T = FINAL_R + 1


def split(value):
    high = value.astype(BF16)
    return high, (value - high.astype(F32)).astype(BF16)


def dot(left, right):
    return jnp.dot(left, right, preferred_element_type=F32)


def split_dot(left, right):
    return dot(left[0], right[0]) + (dot(left[0], right[1]) + dot(left[1], right[0]))


def matmul(left, right):
    return split_dot(split(left), split(right))


def kernel(
    doublings, slabs, incident, down, bounced, settled,
    buf, power, inverse, coupled, field, arrive, leave, handed, handing, extra, pair_t, bounce_t,
    load_sem, store_sem, tree_send, tree_recv, cast_send, cast_recv,
    chain_send, chain_recv, hand_send, hand_recv, extra_send, extra_recv, part_send, part_recv,
    heads, poison, relay_send, relay_recv, give_send, give_recv, last_send, last_recv, swap_send, swap_recv,
    final_send, final_recv,
):
    slab = lax.axis_index("slab")
    depth = lax.axis_index("depth")
    x = lax.rem(slab, 4)
    z = lax.div(slab, 4)
    core = lax.rem(depth, 2)
    y = lax.div(depth, 2)
    chips = lax.axis_size("depth") // 2
    order = buf.shape[1]
    rows = field.shape[0] // CHUNKS
    band = order // CASTS

    loads = [
        pltpu.make_async_copy(slabs.at[0, 0, i], buf.at[OWN + i], load_sem.at[i]) for i in range(4)
    ]
    loads.append(pltpu.make_async_copy(incident.at[0], field, load_sem.at[4]))
    for load in loads:
        load.start()

    def at(px, pz):
        return lax.rem(pz + 16, 8) * 4 + lax.rem(px + 8, 4)

    rt_x = 1 - core
    qu_x = 2 + core

    def slot(level, pair, part):
        return level * 8 + pair * 2 + part

    on_rt = x == rt_x
    on_qu = x == qu_x
    z2 = lax.rem(z, 2)
    z4 = lax.rem(z, 4)
    mirror = at(3 - x, z)
    odd = lax.rem(x, 2) == 1
    beside = at(x + 1 - 2 * lax.rem(x, 2), z)
    takes = on_rt | on_qu
    crossing2 = (on_qu & (z2 == 0)) | (on_rt & (z2 == 1))
    merged2 = (on_rt & (z2 == 0)) | (on_qu & (z2 == 1))
    inner3 = (on_qu & (z4 == 1)) | (on_rt & (z4 == 2))
    ahead3 = jnp.where(z4 < 2, 1, -1)
    near_root, far_root = at(rt_x, NEAR_Z), at(rt_x, FAR_Z)
    is_near = on_rt & (z == NEAR_Z)
    is_far = on_rt & (z == FAR_Z)
    from_qu = on_qu & (z == NEAR_Z + 1)
    root = is_near | is_far

    barrier = pltpu.get_barrier_semaphore()

    def greet(**target):
        pl.semaphore_signal(barrier, inc=1, device_id=target, device_id_type=MESH)

    for px in (1, 3):
        greet(slab=at(x + px, z))
    greet(depth=depth + 1 - 2 * core)

    @pl.when(y > 0)
    def _():
        greet(depth=depth - 2)

    @pl.when(y < chips - 1)
    def _():
        greet(depth=depth + 2)

    meetings = [
        (from_qu, near_root),
        (from_qu, far_root),
        (root, at(qu_x, NEAR_Z + 1)),
        (is_near, far_root),
        (is_far, near_root),
        (z > 0, at(x, z - 1)),
        (z < 7, at(x, z + 1)),
    ]
    for meets, target in meetings:

        @pl.when(meets)
        def _(target=target):
            greet(slab=target)

    met = [y > 0, y < chips - 1] + [meets for meets, _ in meetings]
    pl.semaphore_wait(barrier, 3 + sum(flag.astype(jnp.int32) for flag in met))

    routes = [
        [],
        [(takes, mirror, 2)],
        [
            (crossing2, mirror, 1),
            (crossing2, at(x, z + 1 - 2 * z2), 2),
        ],
        [
            (inner3, mirror, 1),
            (merged2, at(x, z + ahead3), jnp.where(inner3, 2, 0)),
        ],
        [
            (from_qu | is_far, near_root, jnp.where(on_qu, 1, 2)),
            (from_qu | is_near, far_root, jnp.where(on_qu, 1, 0)),
        ],
    ]
    computes = [
        takes,
        takes,
        merged2,
        (on_rt & (z4 == 1)) | (on_qu & (z4 == 2)),
        root,
    ]
    local = [3, 3, 0, 3, 3]
    holds = [is_near, None, is_far]

    def tree_copy(level, number, part, source):
        sends, target, pair = routes[level][number]
        return sends, pltpu.make_async_remote_copy(
            src_ref=buf.at[source],
            dst_ref=buf.at[slot(level, pair, part)],
            send_sem=tree_send.at[level, number, part],
            recv_sem=tree_recv.at[level, pair, part],
            device_id={"slab": target},
            device_id_type=MESH,
        )

    def send_part(level, part, source):
        for number in range(len(routes[level])):
            sends, copy = tree_copy(level, number, part, source)
            if level == 4 and number == 0 and part == 1:
                sends = from_qu

                @pl.when(is_far)
                def _():
                    for piece in range(PIECES):
                        final_copy(piece).start()

            @pl.when(sends)
            def _():
                copy.start()

    def final_copy(piece):
        lines = pl.ds(piece * (order // PIECES), order // PIECES)
        return pltpu.make_async_remote_copy(
            src_ref=buf.at[slot(3, 3, 1), lines],
            dst_ref=buf.at[slot(4, 2, 1), lines],
            send_sem=final_send.at[piece],
            recv_sem=final_recv.at[piece],
            device_id={"slab": near_root},
            device_id_type=MESH,
        )

    def await_part(level, pair, part):
        pltpu.make_async_remote_copy(
            src_ref=buf.at[slot(level, pair, part)],
            dst_ref=buf.at[slot(level, pair, part)],
            send_sem=tree_send.at[level, 0, part],
            recv_sem=tree_recv.at[level, pair, part],
            device_id={"slab": slab},
            device_id_type=MESH,
        ).wait_recv()

    for load in loads[:4]:
        load.wait()
    second = jnp.where(odd == (core == 0), 1, 3)
    blocks = [jnp.where(odd, 0, 2), second, 4 - second, jnp.where(odd, 2, 0)]

    def give_copy(turn):
        return pltpu.make_async_remote_copy(
            src_ref=buf.at[OWN + blocks[turn]],
            dst_ref=buf.at[TAKEN + blocks[turn]],
            send_sem=give_send.at[turn],
            recv_sem=give_recv.at[turn],
            device_id={"slab": beside},
            device_id_type=MESH,
        )

    cut = order // PIECES

    def last_copy(piece):
        lines = pl.ds(piece * cut, cut)
        return pltpu.make_async_remote_copy(
            src_ref=buf.at[OWN + blocks[3], lines],
            dst_ref=buf.at[TAKEN + blocks[3], lines],
            send_sem=last_send.at[piece],
            recv_sem=last_recv.at[piece],
            device_id={"slab": beside},
            device_id_type=MESH,
        )

    def swap_copy(piece):
        lines = pl.ds(piece * cut, cut)
        return pltpu.make_async_remote_copy(
            src_ref=buf.at[slot(0, 3, 0), lines],
            dst_ref=buf.at[slot(1, 2, 0), lines],
            send_sem=swap_send.at[piece],
            recv_sem=swap_recv.at[piece],
            device_id={"slab": mirror},
            device_id_type=MESH,
        )

    @pl.when(jnp.logical_not(takes))
    def _():
        for turn in range(3):
            give_copy(turn).start()
        for piece in range(PIECES):
            last_copy(piece).start()

    head = (pl.ds(0, 8), pl.ds(0, 128))

    def merge(place, wait, finish, transmission_first=False, adds=True, stream=None):
        wait("p1")
        wait("p2")
        near = buf[place["p1"]]
        far = split(buf[place["p2"]])
        system = split_dot(split(near), far)
        ones = lax.broadcasted_iota(jnp.int32, (order, order), 0) == lax.broadcasted_iota(jnp.int32, (order, order), 1)
        inverse[...] = system + jnp.where(ones, 1.0, 0.0)
        power[...] = system

        def double(halves):
            squared = split_dot(halves, halves)
            power[...] = squared
            whole = inverse[...]
            inverse[...] = whole + split_dot(split(squared), split(whole))

        if doublings <= DOUBLINGS:
            for _ in range(doublings - 1):
                double(split(power[...]))
            last = jnp.square(power[...]).reshape(order // 8, 8, order // 128, 128)
            poison[...] = jnp.where(jnp.sum(last, axis=(0, 2)) < REMAINDER / 1024, 0.0, jnp.nan)
        else:

            def step(_, carry):
                double(split(power[...]))
                return carry

            lax.fori_loop(0, doublings - 1, step, 0)
        solved = split(inverse[...])
        coupled[...] = split_dot(far, solved)
        wait("s")
        right = split(buf[place["s"]])
        through = split_dot(solved, right)
        turned = split_dot(split(coupled[...]), right)

        def reflection():
            wait("m1")
            partial = matmul(buf[place["m1"]], turned)
            if adds:
                wait("add")
                partial = buf[place["add"]] + partial
            finish(0, partial)

        def transmission():
            if stream is not None:
                stream(place["m2"], split(through))
                return
            wait("m2")
            finish(1, matmul(buf[place["m2"]], through))

        if transmission_first:
            transmission()
            reflection()
        else:
            reflection()
            transmission()

    def put(place, value):
        buf[place] = value
        if doublings <= DOUBLINGS:
            buf[(place, *head)] += poison[...]

    upper = jnp.where(odd, TAKEN, OWN)
    lower = jnp.where(odd, OWN, TAKEN)

    def sides(is_qu):
        return {
            "p1": jnp.where(is_qu, lower, upper + 2),
            "p2": jnp.where(is_qu, upper + 2, lower),
            "s": jnp.where(is_qu, lower + 3, upper + 1),
            "add": jnp.where(is_qu, lower + 2, upper),
            "m1": jnp.where(is_qu, lower + 1, upper + 3),
            "m2": jnp.where(is_qu, upper + 3, lower + 1),
        }

    def given(turns):
        def wait(name):
            if name in turns:
                if turns[name] < 3:
                    give_copy(turns[name]).wait_recv()
                else:
                    for piece in range(PIECES):
                        last_copy(piece).wait_recv()

        return wait

    def finish_sent(part, value):
        put(slot(0, 3, part), value)
        if part == 1:
            send_part(1, 1, slot(0, 3, 1))
        else:
            for piece in range(PIECES):
                swap_copy(piece).start()

    def finish_pieces(part, value):
        if part == 1:
            finish_sent(part, value)
            return
        put(slot(0, 3, 0), value)
        addend = sides(x < 2)["add"]
        for piece in range(PIECES):
            lines = pl.ds(piece * cut, cut)
            last_copy(piece).wait_recv()
            buf[slot(0, 3, 0), lines] += buf[addend, lines]
            swap_copy(piece).start()

    def finish_kept(part, value):
        put(KEPT + part, value)

    @pl.when(takes & (core == 0))
    def _():
        merge(sides(x < 2), given({"p1": 0, "m2": 1}), finish_sent)
        merge(sides(x >= 2), given({"s": 2, "add": 3}), finish_kept)

    @pl.when(takes & (core == 1))
    def _():
        merge(sides(x < 2), given({"p1": 0, "s": 1, "m1": 2}), finish_pieces, transmission_first=True, adds=False)
        merge(sides(x >= 2), given({}), finish_kept)

    dx = lax.rem(x - rt_x + 4, 4)
    dz = lax.rem(z - NEAR_Z + 4, 4)
    x_first = core == 0
    x_line = jnp.logical_not(x_first) | (dz == 0)
    z_line = x_first | (dx == 0)
    children = [
        (x_line & ((dx == 0) | (x_first & (dx == 1))), at(x + 1, z)),
        (x_line & ((dx == 0) | (jnp.logical_not(x_first) & (dx == 3))), at(x - 1, z)),
        (z_line & (dz <= 1), at(x, z + 1)),
        (z_line & (dz == 0), at(x, z - 1)),
    ]

    def cast_copy(which, chunk, child):
        place = buf.at[FINAL_R + which, pl.ds(chunk * band, band)]
        return pltpu.make_async_remote_copy(
            src_ref=place,
            dst_ref=place,
            send_sem=cast_send.at[which, chunk, child],
            recv_sem=cast_recv.at[which, chunk],
            device_id={"slab": children[child][1]},
            device_id_type=MESH,
        )

    def part_copy(chunk):
        return pltpu.make_async_remote_copy(
            src_ref=buf.at[FINAL_T, pl.ds(chunk * band, band)],
            dst_ref=buf.at[PARTNER, pl.ds(chunk * band, band)],
            send_sem=part_send.at[chunk],
            recv_sem=part_recv.at[chunk],
            device_id={"depth": depth + 1 - 2 * core},
            device_id_type=MESH,
        )

    names = {"add": (0, 0), "s": (0, 1), "p1": (1, 0), "m1": (1, 1), "p2": (2, 0), "m2": (2, 1)}

    def merge_level(level):
        def operand(pair, part):
            if level == 1:
                return [KEPT + part, slot(0, 3, part), slot(1, 2, part)][pair]
            if level == 4:
                return slot(level, 1, part) if pair == 1 else jnp.where(holds[pair], slot(3, 3, part), slot(level, pair, part))
            return slot(level - 1, 3, part) if local[level] == pair else slot(level, pair, part)

        def wait(name):
            pair, part = names[name]
            if level == 4 and pair != 1:

                @pl.when(jnp.logical_not(holds[pair]))
                def _():
                    await_part(level, pair, part)

                return
            if level == 1 and name == "p2":
                for piece in range(PIECES):
                    swap_copy(piece).wait_recv()
            elif pair == 2 if level == 1 else pair != local[level]:
                await_part(level, pair, part)

        def finish(part, value):
            put(slot(level, 3, part), value)
            if level + 1 < LEVELS:
                send_part(level + 1, part, slot(level, 3, part))

        def stream(source, right):
            for piece in range(PIECES):
                lines = pl.ds(piece * cut, cut)

                @pl.when(is_near)
                def _():
                    final_copy(piece).wait_recv()

                buf[FINAL_T, lines] = split_dot(split(buf[source, lines]), right)
                if piece == 0 and doublings <= DOUBLINGS:
                    buf[(FINAL_T, *head)] += poison[...]
                for chunk in range(piece * CASTS // PIECES, (piece + 1) * CASTS // PIECES):
                    for child in range(4):

                        @pl.when(children[child][0])
                        def _():
                            cast_copy(1, chunk, child).start()

        place = {name: operand(*key) for name, key in names.items()}
        last = level + 1 == LEVELS
        merge(place, wait, finish, transmission_first=last, stream=stream if last else None)

    for level in range(1, LEVELS):

        @pl.when(computes[level])
        def _(level=level):
            merge_level(level)

    def relay_copy(way):
        return pltpu.make_async_remote_copy(
            src_ref=heads.at[way],
            dst_ref=heads.at[2 + way],
            send_sem=relay_send.at[way],
            recv_sem=relay_recv.at[way],
            device_id={"depth": lax.rem(depth + (2 * chips - 2 if way else 2), 2 * chips)},
            device_id_type=MESH,
        )

    first = y == 0
    final = y == chips - 1

    def relay(way):
        head = (pl.ds(0, 8), pl.ds(0, 128))
        start, end = (final, first) if way else (first, final)
        heads[way] = (buf[(FINAL_T, *head)] + buf[(PARTNER, *head)]) * 0.0

        @pl.when(jnp.logical_not(start))
        def _():
            relay_copy(way).wait_recv()
            heads[way] += heads[2 + way]

        @pl.when(jnp.logical_not(end))
        def _():
            relay_copy(way).start()

    def forward(which):
        for chunk in range(CASTS):

            @pl.when(jnp.logical_not(root))
            def _():
                cast_copy(which, chunk, 0).wait_recv()

            for child in range(4):

                @pl.when(children[child][0] & jnp.logical_not(root) if which else children[child][0])
                def _():
                    cast_copy(which, chunk, child).start()

            if which == 1:
                part_copy(chunk).start()

    def keep_split(ref, value):
        ref[0], ref[1] = split(value)

    def kept(ref):
        return ref[0], ref[1]

    def forward_r():
        forward(0)
        keep_split(bounce_t, buf[FINAL_R].T)

    extra_copy = pltpu.make_async_remote_copy(
        src_ref=extra,
        dst_ref=extra,
        send_sem=extra_send,
        recv_sem=extra_recv,
        device_id={"depth": depth + 1 - 2 * core},
        device_id_type=MESH,
    )

    def chain_copy(chunk):
        return pltpu.make_async_remote_copy(
            src_ref=leave.at[pl.ds(chunk * rows, rows)],
            dst_ref=arrive.at[pl.ds(chunk * rows, rows)],
            send_sem=chain_send.at[chunk],
            recv_sem=chain_recv.at[chunk],
            device_id={"depth": lax.rem(depth + 2, 2 * chips)},
            device_id_type=MESH,
        )

    def hand_copy(chunk):
        return pltpu.make_async_remote_copy(
            src_ref=field.at[pl.ds(chunk * rows, rows)],
            dst_ref=handed.at[pl.ds(chunk * rows, rows)],
            send_sem=hand_send.at[chunk],
            recv_sem=hand_recv.at[chunk],
            device_id={"depth": depth + 1 - 2 * core},
            device_id_type=MESH,
        )

    forward(1)
    loads[4].wait()

    @pl.when(core == 1)
    def _():
        keep_split(pair_t, buf[FINAL_T].T)
        extra[...] = split_dot(split(field[...]), kept(pair_t))
        extra_copy.start()
        for chunk in range(CASTS):
            part_copy(chunk).wait_recv()
        keep_split(pair_t, buf[PARTNER].T)

        @pl.when(y >= chips // 2)
        def _():
            relay(1)

        forward_r()
        for chunk in range(CHUNKS):
            part = pl.ds(chunk * rows, rows)
            hand_copy(chunk).wait_recv()
            field[part] += split_dot(split(handed[part]), kept(pair_t))

        relay(0)

        @pl.when(y < chips // 2)
        def _():
            relay(1)

    @pl.when(core == 0)
    def _():
        for chunk in range(CASTS):
            part_copy(chunk).wait_recv()
        keep_split(pair_t, matmul(buf[PARTNER], buf[FINAL_T]).T)
        extra_copy.wait_recv()
        extra[...] += split_dot(split(field[...]), kept(pair_t))

        @pl.when(y == 0)
        def _():
            for chunk in range(CHUNKS):
                part = pl.ds(chunk * rows, rows)
                leave[part] = extra[part]
                chain_copy(chunk).start()
                hand_copy(chunk).start()

        @pl.when(y >= chips // 2)
        def _():
            relay(1)

        @pl.when(y > EARLY)
        def _():
            forward_r()

        @pl.when(y > 0)
        def _():
            for chunk in range(CHUNKS):
                part = pl.ds(chunk * rows, rows)
                chain_copy(chunk).wait_recv()

                @pl.when(y < chips - 1)
                def _():
                    leave[part] = extra[part] + split_dot(split(arrive[part]), kept(pair_t))
                    chain_copy(chunk).start()

                field[part] += arrive[part]
                hand_copy(chunk).start()

        relay(0)

        @pl.when(y <= EARLY)
        def _():
            forward_r()

        @pl.when(y < chips // 2)
        def _():
            relay(1)

    store_down = pltpu.make_async_copy(field, down.at[0], store_sem.at[0])
    store_down.start()

    handing[...] = split_dot(split(field[...]), kept(bounce_t))
    store_bounced = pltpu.make_async_copy(handing, bounced.at[0], store_sem.at[1])
    store_bounced.start()

    settled[0, 0] = jnp.sum(heads[0] + heads[1])

    @pl.when(jnp.logical_not(takes))
    def _():
        for turn in range(3):
            give_copy(turn).wait_send()
        for piece in range(PIECES):
            last_copy(piece).wait_send()

    @pl.when(takes)
    def _():
        for piece in range(PIECES):
            swap_copy(piece).wait_send()

    @pl.when(is_far)
    def _():
        for piece in range(PIECES):
            final_copy(piece).wait_send()

    for level in range(LEVELS):
        for number in range(len(routes[level])):
            for part in range(level == 1, 2):
                sends, copy = tree_copy(level, number, part, OWN)
                if level == 4 and number == 0 and part == 1:
                    sends = from_qu

                @pl.when(sends)
                def _():
                    copy.wait_send()

    for which in range(2):
        for chunk in range(CASTS):
            for child in range(4):

                @pl.when(children[child][0])
                def _():
                    cast_copy(which, chunk, child).wait_send()

    for chunk in range(CASTS):
        part_copy(chunk).wait_send()

    @pl.when(core == 1)
    def _():
        extra_copy.wait_send()

    @pl.when(core == 0)
    def _():
        for chunk in range(CHUNKS):
            hand_copy(chunk).wait_send()

        @pl.when(y < chips - 1)
        def _():
            for chunk in range(CHUNKS):
                chain_copy(chunk).wait_send()

    @pl.when(jnp.logical_not(final))
    def _():
        relay_copy(0).wait_send()

    @pl.when(jnp.logical_not(first))
    def _():
        relay_copy(1).wait_send()

    store_down.wait()
    store_bounced.wait()


def layers(doublings, slabs, incident):
    order = slabs.shape[-1]
    rows = incident.shape[1]
    block = jax.ShapeDtypeStruct(incident.shape, F32)
    matrix = pltpu.VMEM((order, order), F32)
    halves = pltpu.VMEM((2, order, order), BF16)
    fields = pltpu.VMEM((rows, order), F32)
    dma = pltpu.SemaphoreType.DMA
    return pl.pallas_call(
        functools.partial(kernel, doublings),
        out_shape=(block, block, jax.ShapeDtypeStruct((1, 1), F32)),
        in_specs=[pl.BlockSpec(memory_space=pl.ANY)] * 2,
        out_specs=[pl.BlockSpec(memory_space=pl.ANY)] * 2 + [pl.BlockSpec(memory_space=pltpu.SMEM)],
        scratch_shapes=[
            pltpu.VMEM((BLOCKS, order, order), F32),
            matrix, matrix, matrix,
            fields, fields, fields, fields, fields, fields,
            halves, halves,
            dma((5,)), dma((2,)),
            dma((LEVELS, 2, 2)), dma((LEVELS, 3, 2)),
            dma((2, CASTS, 4)), dma((2, CASTS)),
            dma((CHUNKS,)), dma((CHUNKS,)),
            dma((CHUNKS,)), dma((CHUNKS,)),
            dma, dma,
            dma((CASTS,)), dma((CASTS,)),
            pltpu.VMEM((4, 8, 128), F32), pltpu.VMEM((8, 128), F32),
            dma((2,)), dma((2,)),
            dma((3,)), dma((3,)), dma((PIECES,)), dma((PIECES,)), dma((PIECES,)), dma((PIECES,)),
            dma((PIECES,)), dma((PIECES,)),
        ],
        compiler_params=pltpu.CompilerParams(
            collective_id=int(doublings > DOUBLINGS), has_side_effects=True, vmem_limit_bytes=60 * 2**20
        ),
        name=f"layers{doublings}",
    )(slabs, incident)


def shards(slabs, incident):
    down, bounced, settled = layers(DOUBLINGS, slabs, incident)
    return lax.cond(
        settled[0, 0] == 0.0,
        lambda: (down, bounced),
        lambda: tuple(layers(MORE_DOUBLINGS, slabs, incident)[:2]),
    )


def solution(mesh):
    placed = (P("depth", "slab", None, None, None), P("depth", "slab", None))
    return jax.shard_map(
        shards,
        mesh=mesh,
        in_specs=placed,
        out_specs=(P("depth", "slab", None), P("depth", "slab", None)),
        check_vma=False,
    )
```

```python
import functools

import jax
import jax.numpy as jnp
from jax import lax
from jax.experimental import pallas as pl
from jax.experimental.pallas import tpu as pltpu
from jax.sharding import PartitionSpec as P

F32 = jnp.float32
BF16 = jnp.bfloat16
MESH = pl.DeviceIdType.MESH
DOUBLINGS = 3
MORE_DOUBLINGS = 24
REMAINDER = 1e-5
CHUNKS = 8
CASTS = 8
NEAR_Z = 1
PIECES = 4
FAR_Z = 5
EARLY = 1
LEVELS = 5
OWN = 8 * LEVELS
PARTNER = OWN + 4
BLOCKS = OWN + 5
TAKEN = 2
KEPT = 0
FINAL_R = 8 * (LEVELS - 1) + 6
FINAL_T = FINAL_R + 1


def split(value):
    high = value.astype(BF16)
    return high, (value - high.astype(F32)).astype(BF16)


def dot(left, right):
    return jnp.dot(left, right, preferred_element_type=F32)


def split_dot(left, right):
    return dot(left[0], right[0]) + (dot(left[0], right[1]) + dot(left[1], right[0]))


def matmul(left, right):
    return split_dot(split(left), split(right))


def kernel(
    doublings, slabs, incident, down, bounced, settled,
    buf, power, inverse, coupled, field, arrive, leave, handed, handing, extra, pair_t, bounce_t,
    load_sem, store_sem, tree_send, tree_recv, cast_send, cast_recv,
    chain_send, chain_recv, hand_send, hand_recv, extra_send, extra_recv, part_send, part_recv,
    heads, poison, relay_send, relay_recv, give_send, give_recv, last_send, last_recv, swap_send, swap_recv,
    final_send, final_recv,
):
    slab = lax.axis_index("slab")
    depth = lax.axis_index("depth")
    x = lax.rem(slab, 4)
    z = lax.div(slab, 4)
    core = lax.rem(depth, 2)
    y = lax.div(depth, 2)
    chips = lax.axis_size("depth") // 2
    order = buf.shape[1]
    rows = field.shape[0] // CHUNKS
    band = order // CASTS

    loads = [
        pltpu.make_async_copy(slabs.at[0, 0, i], buf.at[OWN + i], load_sem.at[i]) for i in range(4)
    ]
    loads.append(pltpu.make_async_copy(incident.at[0], field, load_sem.at[4]))
    for load in loads:
        load.start()

    def at(px, pz):
        return lax.rem(pz + 16, 8) * 4 + lax.rem(px + 8, 4)

    rt_x = 1 - core
    qu_x = 2 + core

    def slot(level, pair, part):
        return level * 8 + pair * 2 + part

    on_rt = x == rt_x
    on_qu = x == qu_x
    z2 = lax.rem(z, 2)
    z4 = lax.rem(z, 4)
    mirror = at(3 - x, z)
    odd = lax.rem(x, 2) == 1
    beside = at(x + 1 - 2 * lax.rem(x, 2), z)
    takes = on_rt | on_qu
    crossing2 = (on_qu & (z2 == 0)) | (on_rt & (z2 == 1))
    merged2 = (on_rt & (z2 == 0)) | (on_qu & (z2 == 1))
    inner3 = (on_qu & (z4 == 1)) | (on_rt & (z4 == 2))
    ahead3 = jnp.where(z4 < 2, 1, -1)
    near_root, far_root = at(rt_x, NEAR_Z), at(rt_x, FAR_Z)
    is_near = on_rt & (z == NEAR_Z)
    is_far = on_rt & (z == FAR_Z)
    from_qu = on_qu & (z == NEAR_Z + 1)
    root = is_near | is_far

    barrier = pltpu.get_barrier_semaphore()

    def greet(**target):
        pl.semaphore_signal(barrier, inc=1, device_id=target, device_id_type=MESH)

    for px in (1, 3):
        greet(slab=at(x + px, z))
    greet(depth=depth + 1 - 2 * core)

    @pl.when(y > 0)
    def _():
        greet(depth=depth - 2)

    @pl.when(y < chips - 1)
    def _():
        greet(depth=depth + 2)

    meetings = [
        (from_qu, near_root),
        (from_qu, far_root),
        (root, at(qu_x, NEAR_Z + 1)),
        (is_near, far_root),
        (is_far, near_root),
        (z > 0, at(x, z - 1)),
        (z < 7, at(x, z + 1)),
    ]
    for meets, target in meetings:

        @pl.when(meets)
        def _(target=target):
            greet(slab=target)

    met = [y > 0, y < chips - 1] + [meets for meets, _ in meetings]
    pl.semaphore_wait(barrier, 3 + sum(flag.astype(jnp.int32) for flag in met))

    routes = [
        [],
        [(takes, mirror, 2)],
        [
            (crossing2, mirror, 1),
            (crossing2, at(x, z + 1 - 2 * z2), 2),
        ],
        [
            (inner3, mirror, 1),
            (merged2, at(x, z + ahead3), jnp.where(inner3, 2, 0)),
        ],
        [
            (from_qu | is_far, near_root, jnp.where(on_qu, 1, 2)),
            (from_qu | is_near, far_root, jnp.where(on_qu, 1, 0)),
        ],
    ]
    computes = [
        takes,
        takes,
        merged2,
        (on_rt & (z4 == 1)) | (on_qu & (z4 == 2)),
        root,
    ]
    local = [3, 3, 0, 3, 3]
    holds = [is_near, None, is_far]

    def tree_copy(level, number, part, source):
        sends, target, pair = routes[level][number]
        return sends, pltpu.make_async_remote_copy(
            src_ref=buf.at[source],
            dst_ref=buf.at[slot(level, pair, part)],
            send_sem=tree_send.at[level, number, part],
            recv_sem=tree_recv.at[level, pair, part],
            device_id={"slab": target},
            device_id_type=MESH,
        )

    def send_part(level, part, source):
        for number in range(len(routes[level])):
            sends, copy = tree_copy(level, number, part, source)
            if level == 4 and number == 0 and part == 1:
                sends = from_qu

                @pl.when(is_far)
                def _():
                    for piece in range(PIECES):
                        final_copy(piece).start()

            @pl.when(sends)
            def _():
                copy.start()

    def final_copy(piece):
        lines = pl.ds(piece * (order // PIECES), order // PIECES)
        return pltpu.make_async_remote_copy(
            src_ref=buf.at[slot(3, 3, 1), lines],
            dst_ref=buf.at[slot(4, 2, 1), lines],
            send_sem=final_send.at[piece],
            recv_sem=final_recv.at[piece],
            device_id={"slab": near_root},
            device_id_type=MESH,
        )

    def await_part(level, pair, part):
        pltpu.make_async_remote_copy(
            src_ref=buf.at[slot(level, pair, part)],
            dst_ref=buf.at[slot(level, pair, part)],
            send_sem=tree_send.at[level, 0, part],
            recv_sem=tree_recv.at[level, pair, part],
            device_id={"slab": slab},
            device_id_type=MESH,
        ).wait_recv()

    for load in loads[:4]:
        load.wait()
    second = jnp.where(odd == (core == 0), 1, 3)
    blocks = [jnp.where(odd, 0, 2), second, 4 - second, jnp.where(odd, 2, 0)]

    def give_copy(turn):
        return pltpu.make_async_remote_copy(
            src_ref=buf.at[OWN + blocks[turn]],
            dst_ref=buf.at[TAKEN + blocks[turn]],
            send_sem=give_send.at[turn],
            recv_sem=give_recv.at[turn],
            device_id={"slab": beside},
            device_id_type=MESH,
        )

    cut = order // PIECES

    def last_copy(piece):
        lines = pl.ds(piece * cut, cut)
        return pltpu.make_async_remote_copy(
            src_ref=buf.at[OWN + blocks[3], lines],
            dst_ref=buf.at[TAKEN + blocks[3], lines],
            send_sem=last_send.at[piece],
            recv_sem=last_recv.at[piece],
            device_id={"slab": beside},
            device_id_type=MESH,
        )

    def swap_copy(piece):
        lines = pl.ds(piece * cut, cut)
        return pltpu.make_async_remote_copy(
            src_ref=buf.at[slot(0, 3, 0), lines],
            dst_ref=buf.at[slot(1, 2, 0), lines],
            send_sem=swap_send.at[piece],
            recv_sem=swap_recv.at[piece],
            device_id={"slab": mirror},
            device_id_type=MESH,
        )

    @pl.when(jnp.logical_not(takes))
    def _():
        for turn in range(3):
            give_copy(turn).start()
        for piece in range(PIECES):
            last_copy(piece).start()

    head = (pl.ds(0, 8), pl.ds(0, 128))

    def merge(place, wait, finish, transmission_first=False, adds=True, stream=None):
        wait("p1")
        wait("p2")
        near = buf[place["p1"]]
        far = split(buf[place["p2"]])
        system = split_dot(split(near), far)
        ones = lax.broadcasted_iota(jnp.int32, (order, order), 0) == lax.broadcasted_iota(jnp.int32, (order, order), 1)
        inverse[...] = system + jnp.where(ones, 1.0, 0.0)
        power[...] = system

        def double(halves):
            squared = split_dot(halves, halves)
            power[...] = squared
            whole = inverse[...]
            inverse[...] = whole + split_dot(split(squared), split(whole))

        if doublings <= DOUBLINGS:
            for _ in range(doublings - 1):
                double(split(power[...]))
            last = jnp.square(power[...]).reshape(order // 8, 8, order // 128, 128)
            poison[...] = jnp.where(jnp.sum(last, axis=(0, 2)) < REMAINDER / 1024, 0.0, jnp.nan)
        else:

            def step(_, carry):
                double(split(power[...]))
                return carry

            lax.fori_loop(0, doublings - 1, step, 0)
        solved = split(inverse[...])
        coupled[...] = split_dot(far, solved)
        wait("s")
        right = split(buf[place["s"]])
        through = split_dot(solved, right)
        turned = split_dot(split(coupled[...]), right)

        def reflection():
            wait("m1")
            partial = matmul(buf[place["m1"]], turned)
            if adds:
                wait("add")
                partial = buf[place["add"]] + partial
            finish(0, partial)

        def transmission():
            if stream is not None:
                stream(place["m2"], split(through))
                return
            wait("m2")
            finish(1, matmul(buf[place["m2"]], through))

        if transmission_first:
            transmission()
            reflection()
        else:
            reflection()
            transmission()

    def put(place, value):
        buf[place] = value
        if doublings <= DOUBLINGS:
            buf[(place, *head)] += poison[...]

    upper = jnp.where(odd, TAKEN, OWN)
    lower = jnp.where(odd, OWN, TAKEN)

    def sides(is_qu):
        return {
            "p1": jnp.where(is_qu, lower, upper + 2),
            "p2": jnp.where(is_qu, upper + 2, lower),
            "s": jnp.where(is_qu, lower + 3, upper + 1),
            "add": jnp.where(is_qu, lower + 2, upper),
            "m1": jnp.where(is_qu, lower + 1, upper + 3),
            "m2": jnp.where(is_qu, upper + 3, lower + 1),
        }

    def given(turns):
        def wait(name):
            if name in turns:
                if turns[name] < 3:
                    give_copy(turns[name]).wait_recv()
                else:
                    for piece in range(PIECES):
                        last_copy(piece).wait_recv()

        return wait

    def finish_sent(part, value):
        put(slot(0, 3, part), value)
        if part == 1:
            send_part(1, 1, slot(0, 3, 1))
        else:
            for piece in range(PIECES):
                swap_copy(piece).start()

    def finish_pieces(part, value):
        if part == 1:
            finish_sent(part, value)
            return
        put(slot(0, 3, 0), value)
        addend = sides(x < 2)["add"]
        for piece in range(PIECES):
            lines = pl.ds(piece * cut, cut)
            last_copy(piece).wait_recv()
            buf[slot(0, 3, 0), lines] += buf[addend, lines]
            swap_copy(piece).start()

    def finish_kept(part, value):
        put(KEPT + part, value)

    @pl.when(takes & (core == 0))
    def _():
        merge(sides(x < 2), given({"p1": 0, "m2": 1}), finish_sent)
        merge(sides(x >= 2), given({"s": 2, "add": 3}), finish_kept)

    @pl.when(takes & (core == 1))
    def _():
        merge(sides(x < 2), given({"p1": 0, "s": 1, "m1": 2}), finish_pieces, transmission_first=True, adds=False)
        merge(sides(x >= 2), given({}), finish_kept)

    dx = lax.rem(x - rt_x + 4, 4)
    dz = lax.rem(z - NEAR_Z + 4, 4)
    x_first = core == 0
    x_line = jnp.logical_not(x_first) | (dz == 0)
    z_line = x_first | (dx == 0)
    children = [
        (x_line & ((dx == 0) | (x_first & (dx == 1))), at(x + 1, z)),
        (x_line & ((dx == 0) | (jnp.logical_not(x_first) & (dx == 3))), at(x - 1, z)),
        (z_line & (dz <= 1), at(x, z + 1)),
        (z_line & (dz == 0), at(x, z - 1)),
    ]

    def cast_copy(which, chunk, child):
        place = buf.at[FINAL_R + which, pl.ds(chunk * band, band)]
        return pltpu.make_async_remote_copy(
            src_ref=place,
            dst_ref=place,
            send_sem=cast_send.at[which, chunk, child],
            recv_sem=cast_recv.at[which, chunk],
            device_id={"slab": children[child][1]},
            device_id_type=MESH,
        )

    def part_copy(chunk):
        return pltpu.make_async_remote_copy(
            src_ref=buf.at[FINAL_T, pl.ds(chunk * band, band)],
            dst_ref=buf.at[PARTNER, pl.ds(chunk * band, band)],
            send_sem=part_send.at[chunk],
            recv_sem=part_recv.at[chunk],
            device_id={"depth": depth + 1 - 2 * core},
            device_id_type=MESH,
        )

    names = {"add": (0, 0), "s": (0, 1), "p1": (1, 0), "m1": (1, 1), "p2": (2, 0), "m2": (2, 1)}

    def merge_level(level):
        def operand(pair, part):
            if level == 1:
                return [KEPT + part, slot(0, 3, part), slot(1, 2, part)][pair]
            if level == 4:
                return slot(level, 1, part) if pair == 1 else jnp.where(holds[pair], slot(3, 3, part), slot(level, pair, part))
            return slot(level - 1, 3, part) if local[level] == pair else slot(level, pair, part)

        def wait(name):
            pair, part = names[name]
            if level == 4 and pair != 1:

                @pl.when(jnp.logical_not(holds[pair]))
                def _():
                    await_part(level, pair, part)

                return
            if level == 1 and name == "p2":
                for piece in range(PIECES):
                    swap_copy(piece).wait_recv()
            elif pair == 2 if level == 1 else pair != local[level]:
                await_part(level, pair, part)

        def finish(part, value):
            put(slot(level, 3, part), value)
            if level + 1 < LEVELS:
                send_part(level + 1, part, slot(level, 3, part))

        def stream(source, right):
            for piece in range(PIECES):
                lines = pl.ds(piece * cut, cut)

                @pl.when(is_near)
                def _():
                    final_copy(piece).wait_recv()

                buf[FINAL_T, lines] = split_dot(split(buf[source, lines]), right)
                if piece == 0 and doublings <= DOUBLINGS:
                    buf[(FINAL_T, *head)] += poison[...]
                for chunk in range(piece * CASTS // PIECES, (piece + 1) * CASTS // PIECES):
                    for child in range(4):

                        @pl.when(children[child][0])
                        def _():
                            cast_copy(1, chunk, child).start()

        place = {name: operand(*key) for name, key in names.items()}
        last = level + 1 == LEVELS
        merge(place, wait, finish, transmission_first=last, stream=stream if last else None)

    for level in range(1, LEVELS):

        @pl.when(computes[level])
        def _(level=level):
            merge_level(level)

    def relay_copy(way):
        return pltpu.make_async_remote_copy(
            src_ref=heads.at[way],
            dst_ref=heads.at[2 + way],
            send_sem=relay_send.at[way],
            recv_sem=relay_recv.at[way],
            device_id={"depth": lax.rem(depth + (2 * chips - 2 if way else 2), 2 * chips)},
            device_id_type=MESH,
        )

    first = y == 0
    final = y == chips - 1

    def relay(way):
        head = (pl.ds(0, 8), pl.ds(0, 128))
        start, end = (final, first) if way else (first, final)
        heads[way] = (buf[(FINAL_T, *head)] + buf[(PARTNER, *head)]) * 0.0

        @pl.when(jnp.logical_not(start))
        def _():
            relay_copy(way).wait_recv()
            heads[way] += heads[2 + way]

        @pl.when(jnp.logical_not(end))
        def _():
            relay_copy(way).start()

    def forward(which):
        for chunk in range(CASTS):

            @pl.when(jnp.logical_not(root))
            def _():
                cast_copy(which, chunk, 0).wait_recv()

            for child in range(4):

                @pl.when(children[child][0] & jnp.logical_not(root) if which else children[child][0])
                def _():
                    cast_copy(which, chunk, child).start()

            if which == 1:
                part_copy(chunk).start()

    def keep_split(ref, value):
        ref[0], ref[1] = split(value)

    def kept(ref):
        return ref[0], ref[1]

    def forward_r():
        forward(0)
        keep_split(bounce_t, buf[FINAL_R].T)

    extra_copy = pltpu.make_async_remote_copy(
        src_ref=extra,
        dst_ref=extra,
        send_sem=extra_send,
        recv_sem=extra_recv,
        device_id={"depth": depth + 1 - 2 * core},
        device_id_type=MESH,
    )

    def chain_copy(chunk):
        return pltpu.make_async_remote_copy(
            src_ref=leave.at[pl.ds(chunk * rows, rows)],
            dst_ref=arrive.at[pl.ds(chunk * rows, rows)],
            send_sem=chain_send.at[chunk],
            recv_sem=chain_recv.at[chunk],
            device_id={"depth": lax.rem(depth + 2, 2 * chips)},
            device_id_type=MESH,
        )

    def hand_copy(chunk):
        return pltpu.make_async_remote_copy(
            src_ref=field.at[pl.ds(chunk * rows, rows)],
            dst_ref=handed.at[pl.ds(chunk * rows, rows)],
            send_sem=hand_send.at[chunk],
            recv_sem=hand_recv.at[chunk],
            device_id={"depth": depth + 1 - 2 * core},
            device_id_type=MESH,
        )

    forward(1)
    loads[4].wait()

    @pl.when(core == 1)
    def _():
        keep_split(pair_t, buf[FINAL_T].T)
        extra[...] = split_dot(split(field[...]), kept(pair_t))
        extra_copy.start()
        for chunk in range(CASTS):
            part_copy(chunk).wait_recv()
        keep_split(pair_t, buf[PARTNER].T)

        @pl.when(y >= chips // 2)
        def _():
            relay(1)

        forward_r()
        for chunk in range(CHUNKS):
            part = pl.ds(chunk * rows, rows)
            hand_copy(chunk).wait_recv()
            field[part] += split_dot(split(handed[part]), kept(pair_t))

        relay(0)

        @pl.when(y < chips // 2)
        def _():
            relay(1)

    @pl.when(core == 0)
    def _():
        for chunk in range(CASTS):
            part_copy(chunk).wait_recv()
        keep_split(pair_t, matmul(buf[PARTNER], buf[FINAL_T]).T)
        extra_copy.wait_recv()
        extra[...] += split_dot(split(field[...]), kept(pair_t))

        @pl.when(y == 0)
        def _():
            for chunk in range(CHUNKS):
                part = pl.ds(chunk * rows, rows)
                leave[part] = extra[part]
                chain_copy(chunk).start()
                hand_copy(chunk).start()

        @pl.when(y >= chips // 2)
        def _():
            relay(1)

        @pl.when(y > EARLY)
        def _():
            forward_r()

        @pl.when(y > 0)
        def _():
            for chunk in range(CHUNKS):
                part = pl.ds(chunk * rows, rows)
                chain_copy(chunk).wait_recv()

                @pl.when(y < chips - 1)
                def _():
                    leave[part] = extra[part] + split_dot(split(arrive[part]), kept(pair_t))
                    chain_copy(chunk).start()

                field[part] += arrive[part]
                hand_copy(chunk).start()

        relay(0)

        @pl.when(y <= EARLY)
        def _():
            forward_r()

        @pl.when(y < chips // 2)
        def _():
            relay(1)

    store_down = pltpu.make_async_copy(field, down.at[0], store_sem.at[0])
    store_down.start()

    handing[...] = split_dot(split(field[...]), kept(bounce_t))
    store_bounced = pltpu.make_async_copy(handing, bounced.at[0], store_sem.at[1])
    store_bounced.start()

    settled[0, 0] = jnp.sum(heads[0] + heads[1])

    @pl.when(jnp.logical_not(takes))
    def _():
        for turn in range(3):
            give_copy(turn).wait_send()
        for piece in range(PIECES):
            last_copy(piece).wait_send()

    @pl.when(takes)
    def _():
        for piece in range(PIECES):
            swap_copy(piece).wait_send()

    @pl.when(is_far)
    def _():
        for piece in range(PIECES):
            final_copy(piece).wait_send()

    for level in range(LEVELS):
        for number in range(len(routes[level])):
            for part in range(level == 1, 2):
                sends, copy = tree_copy(level, number, part, OWN)
                if level == 4 and number == 0 and part == 1:
                    sends = from_qu

                @pl.when(sends)
                def _():
                    copy.wait_send()

    for which in range(2):
        for chunk in range(CASTS):
            for child in range(4):

                @pl.when(children[child][0])
                def _():
                    cast_copy(which, chunk, child).wait_send()

    for chunk in range(CASTS):
        part_copy(chunk).wait_send()

    @pl.when(core == 1)
    def _():
        extra_copy.wait_send()

    @pl.when(core == 0)
    def _():
        for chunk in range(CHUNKS):
            hand_copy(chunk).wait_send()

        @pl.when(y < chips - 1)
        def _():
            for chunk in range(CHUNKS):
                chain_copy(chunk).wait_send()

    @pl.when(jnp.logical_not(final))
    def _():
        relay_copy(0).wait_send()

    @pl.when(jnp.logical_not(first))
    def _():
        relay_copy(1).wait_send()

    store_down.wait()
    store_bounced.wait()


def layers(doublings, slabs, incident):
    order = slabs.shape[-1]
    rows = incident.shape[1]
    block = jax.ShapeDtypeStruct(incident.shape, F32)
    matrix = pltpu.VMEM((order, order), F32)
    halves = pltpu.VMEM((2, order, order), BF16)
    fields = pltpu.VMEM((rows, order), F32)
    dma = pltpu.SemaphoreType.DMA
    return pl.pallas_call(
        functools.partial(kernel, doublings),
        out_shape=(block, block, jax.ShapeDtypeStruct((1, 1), F32)),
        in_specs=[pl.BlockSpec(memory_space=pl.ANY)] * 2,
        out_specs=[pl.BlockSpec(memory_space=pl.ANY)] * 2 + [pl.BlockSpec(memory_space=pltpu.SMEM)],
        scratch_shapes=[
            pltpu.VMEM((BLOCKS, order, order), F32),
            matrix, matrix, matrix,
            fields, fields, fields, fields, fields, fields,
            halves, halves,
            dma((5,)), dma((2,)),
            dma((LEVELS, 2, 2)), dma((LEVELS, 3, 2)),
            dma((2, CASTS, 4)), dma((2, CASTS)),
            dma((CHUNKS,)), dma((CHUNKS,)),
            dma((CHUNKS,)), dma((CHUNKS,)),
            dma, dma,
            dma((CASTS,)), dma((CASTS,)),
            pltpu.VMEM((4, 8, 128), F32), pltpu.VMEM((8, 128), F32),
            dma((2,)), dma((2,)),
            dma((3,)), dma((3,)), dma((PIECES,)), dma((PIECES,)), dma((PIECES,)), dma((PIECES,)),
            dma((PIECES,)), dma((PIECES,)),
        ],
        compiler_params=pltpu.CompilerParams(
            collective_id=int(doublings > DOUBLINGS), has_side_effects=True, vmem_limit_bytes=60 * 2**20
        ),
        name=f"layers{doublings}",
    )(slabs, incident)


def shards(slabs, incident):
    down, bounced, settled = layers(DOUBLINGS, slabs, incident)
    return lax.cond(
        settled[0, 0] == 0.0,
        lambda: (down, bounced),
        lambda: tuple(layers(MORE_DOUBLINGS, slabs, incident)[:2]),
    )


def solution(mesh):
    placed = (P("depth", "slab", None, None, None), P("depth", "slab", None))
    return jax.shard_map(
        shards,
        mesh=mesh,
        in_specs=placed,
        out_specs=(P("depth", "slab", None), P("depth", "slab", None)),
        check_vma=False,
    )
```
